512 devices in a mesh: hist: 16 (over y, x_hi, core), item: 32 (over z, x_lo).
Axes of the slice: x: 4 (x_hi: 2, x_lo: 2; x = x_hi * 2 + x_lo), y: 4, z: 16, core: 2. Of those that a mesh axis runs over, the one named last changes fastest.
Arguments:
- events: bfloat16 [32, 16384, 512], P('item', 'hist'), may hold values from -6 to 6
- item_ids: int32 [32, 16384], P('item', 'hist'), may hold values from 0 to 524287
- lengths: int32 [32], P('item'), may hold values from 4096 to 16384, as said below
- w_proj: bfloat16 [512, 2048], replicated, may hold values from -0.25 to 0.25
- w_out: bfloat16 [512, 512], replicated, may hold values from -0.25 to 0.25
- repeat_bias: float32 [4], replicated, may hold values from 1 to 3
- item_slab: bfloat16 [524288, 512], P(('hist', 'item')), as said below
Outputs:
- log_probs: float32 [32, 524288], P(None, ('hist', 'item'))
The draws below stay inside these ranges and needn't reach their ends.
Inputs may be any that keep to these rules, and one draw needn't show every extreme that they name: `lengths`: some user's history is fully valid in every draw. `item_slab`: entries lie within -240 / sqrt(512) and 240 / sqrt(512).
All inputs are finite; a program needn't handle non-finite values.
Results may differ from the reference program's by a relative error of at most 0.00075.
Values may be sent and summed in bfloat16 or wider, within the bound.
No kernel may reach another device: no remote copies, remote signals or barrier semaphores. Data moves between devices by JAX's collectives and lax.ppermute only.
A program may use at most 64 MiB of HBM per device.

```python
import math
import jax
import jax.numpy as jnp
import numpy as np
from jax import lax

D = 512
HEADS = 4
WINDOW = 1024
L_DEV = 1024
HISTORY = 16384
USERS = 32
ITEMS = 524288


def draw_lengths(key, part):
    first_key, second_key = jax.random.split(jax.random.fold_in(key, 11))
    drawn = jax.random.randint(first_key, (USERS,), HISTORY // 4, HISTORY + 1)
    chosen = jax.random.randint(second_key, (), 0, USERS)
    return jnp.where(jnp.arange(USERS) == chosen, HISTORY, drawn).astype(jnp.int32)


def draw_item_slab(key, part):
    first_key = jax.random.fold_in(jax.random.fold_in(key, 23), 0)
    base = jnp.clip(jax.random.normal(first_key, (ITEMS, D), jnp.float32), -6.0, 6.0) / math.sqrt(D)
    return base.astype(jnp.bfloat16)


def place_ends(values, rng, smallest, largest):
    shape = values.shape
    spot = [jax.random.randint(jax.random.fold_in(rng, axis), (), 0, shape[axis]) for axis in range(len(shape))]
    values = values.at[tuple(spot)].set(smallest)
    longest = shape.index(max(shape))
    spot[longest] = (spot[longest] + 1) % shape[longest]
    return values.at[tuple(spot)].set(largest)


def levels(rng, extent, cuts, low, high):
    loudness, own = 1.0, jax.random.fold_in(rng, 6)
    for dim, blocks in cuts:
        heights = jnp.exp(jax.random.uniform(jax.random.fold_in(own, dim), (blocks,), jnp.float32, low / len(cuts), high / len(cuts)))
        loudness = loudness * jnp.repeat(heights, extent[dim] // blocks).reshape([-1 if axis == dim else 1 for axis in range(len(extent))])
    return loudness


def skewed_wide(stream_key, shape, count, slope):
    portions = [min(1 << octave, count + 1 - (1 << octave)) * (1 << 20) // math.isqrt((1 << octave) ** slope) + 1 for octave in range((count + 1).bit_length()) if 1 << octave <= count]
    spread = 1 + sum(portions) // (1 << 30)
    listing = np.cumsum(np.array([max(1, weight // spread) for weight in portions]))
    lot = jax.random.randint(jax.random.fold_in(stream_key, 1), shape, 0, int(listing[len(portions) - 1]))
    start = jnp.left_shift(1, jnp.searchsorted(jnp.asarray(listing, jnp.int32), lot, side="right").astype(jnp.int32))
    rank = start - 1 + jax.random.randint(jax.random.fold_in(stream_key, 4), shape, 0, 1 << 30) % jnp.minimum(start, count + 1 - start)
    return jax.random.permutation(jax.random.fold_in(stream_key, 2), count)[rank].astype(jnp.int32)


def bell_draw(rng, extent, spread, limit, cuts=(), kind=jnp.bfloat16):
    array = jax.random.normal(rng, extent, jnp.float32) * spread
    if len(cuts) > 0:
        array = levels(rng, extent, cuts, -0.22, 0.18) * array
    return jnp.clip(array, min=-limit, max=limit).astype(kind)


def setup_inputs(seed: int = 0) -> dict:
    arg_keys = jax.random.split(jax.random.key(seed), 8)
    events = bell_draw(arg_keys[0], (USERS, HISTORY, D), 1.0, 6.0, ((0, 32), (1, 16)))
    item_ids = place_ends(skewed_wide(arg_keys[1], (USERS, HISTORY), ITEMS, 3), jax.random.fold_in(arg_keys[1], 3), 0, ITEMS - 1).astype(jnp.int32)
    lengths = draw_lengths(jax.random.fold_in(arg_keys[7], 71), 0)
    w_proj = bell_draw(arg_keys[3], (D, 4 * D), D ** -0.5, 0.25)
    w_out = bell_draw(arg_keys[4], (D, D), D ** -0.5, 0.25)
    repeat_bias = jnp.clip(jax.random.uniform(arg_keys[5], (HEADS,), jnp.float32, 1.0, 3.0), 1.0, 3.0)
    item_slab = draw_item_slab(jax.random.fold_in(arg_keys[7], 71), 0)
    return {"events": events, "item_ids": item_ids, "lengths": lengths, "w_proj": w_proj, "w_out": w_out, "repeat_bias": repeat_bias, "item_slab": item_slab}


def block_pool(first_row, x_rows, gate_part, query_part, key_cat, value_cat, id_rows, id_cat, length, w_out, repeat_bias, block_rows):
    head_count = repeat_bias.shape[0]
    head_dim = D // head_count
    queries = lax.dynamic_slice_in_dim(query_part, first_row, block_rows, 0).astype(jnp.float32).reshape(block_rows, head_count, head_dim)
    key_rows = lax.dynamic_slice_in_dim(key_cat, first_row, block_rows + WINDOW, 0).astype(jnp.float32).reshape(block_rows + WINDOW, head_count, head_dim)
    value_rows = lax.dynamic_slice_in_dim(value_cat, first_row, block_rows + WINDOW, 0).astype(jnp.float32).reshape(block_rows + WINDOW, head_count, head_dim)
    query_ids = lax.dynamic_slice_in_dim(id_rows, first_row, block_rows, 0)
    key_ids = lax.dynamic_slice_in_dim(id_cat, first_row, block_rows + WINDOW, 0)
    scores = jnp.einsum('qhd,khd->hqk', queries, key_rows) * (1.0 / math.sqrt(head_dim))
    same_item = (query_ids[:, None] == key_ids[None, :]).astype(jnp.float32)
    scores = scores + repeat_bias[:, None, None] * same_item[None]
    row_index = jnp.arange(block_rows, dtype=jnp.int32)[:, None]
    col_index = jnp.arange(block_rows + WINDOW, dtype=jnp.int32)[None, :]
    key_pos = first_row + col_index - WINDOW
    valid_mask = (col_index >= row_index + 1) & (col_index <= row_index + WINDOW) & (key_pos >= 0) & (key_pos < length)
    weights = (jnp.where(valid_mask[None], jax.nn.silu(scores), 0.0) / WINDOW).astype(jnp.bfloat16)
    mixed = jnp.einsum('hqk,khd->qhd', weights.astype(jnp.float32), value_rows).reshape(block_rows, D)
    centered = mixed - lax.optimization_barrier(jnp.mean(mixed, axis=1, keepdims=True))
    normed = centered * lax.rsqrt(lax.optimization_barrier(jnp.mean(centered * centered, axis=1, keepdims=True)) + 1e-06)
    gate_rows = lax.dynamic_slice_in_dim(gate_part, first_row, block_rows, 0)
    gated_rows = (normed * gate_rows.astype(jnp.float32)).astype(jnp.bfloat16)
    x_block = lax.dynamic_slice_in_dim(x_rows, first_row, block_rows, 0)
    layer_out = jnp.dot(gated_rows, w_out, preferred_element_type=jnp.float32) + x_block.astype(jnp.float32)
    query_pos = first_row + jnp.arange(block_rows, dtype=jnp.int32)
    return lax.optimization_barrier(jnp.sum(jnp.where((query_pos < length)[:, None], layer_out, 0.0), axis=0))

def reference(events, item_ids, lengths, w_proj, w_out, repeat_bias, item_slab):
    block_rows = min(256, L_DEV)
    block_count = HISTORY // block_rows

    def per_user(packed):
        x_rows, id_rows, length = packed
        projected = jax.nn.silu(jnp.dot(x_rows, w_proj, preferred_element_type=jnp.float32)).astype(jnp.bfloat16)
        gate_part = projected[:, :D]
        value_part = projected[:, D:2 * D]
        query_part = projected[:, 2 * D:3 * D]
        key_part = projected[:, 3 * D:]
        key_cat = jnp.concatenate([jnp.zeros((WINDOW, D), jnp.bfloat16), key_part], axis=0)
        value_cat = jnp.concatenate([jnp.zeros((WINDOW, D), jnp.bfloat16), value_part], axis=0)
        id_cat = jnp.concatenate([jnp.zeros((WINDOW,), jnp.int32), id_rows.astype(jnp.int32)], axis=0)

        def one_block(first_row):
            return block_pool(first_row, x_rows, gate_part, query_part, key_cat, value_cat, id_rows, id_cat, length, w_out, repeat_bias, block_rows)
        starts = jnp.arange(block_count, dtype=jnp.int32) * block_rows
        return lax.optimization_barrier(jnp.sum(lax.map(one_block, starts), axis=0))
    pooled = lax.map(per_user, (events, item_ids, lengths))
    user_vecs = (pooled * lax.rsqrt(lax.optimization_barrier(jnp.mean(pooled * pooled, axis=1, keepdims=True)) + 1e-06)).astype(jnp.bfloat16)
    logits = 4.0 * jnp.dot(user_vecs, item_slab.T, preferred_element_type=jnp.float32)
    top_logit = lax.optimization_barrier(jnp.max(logits, axis=1))
    exp_total = lax.optimization_barrier(jnp.sum(jnp.exp(logits - top_logit[:, None]), axis=1))
    return logits - (top_logit + jnp.log(exp_total))[:, None]
```

```python
import functools
import math

import jax
import jax.numpy as jnp
from jax import lax
from jax.experimental import pallas as pl
from jax.experimental.pallas import tpu as pltpu
from jax.sharding import PartitionSpec as P

WINDOW = 1024
BLOCK = 256
NT = (((1,), (1,)), ((), ()))


def mm(a, b):
    return jnp.dot(a, b, preferred_element_type=jnp.float32)


def silu(x):
    half = 0.5 * x
    return half * jnp.tanh(half) + half


def spread_ids(ids_ref, out_ref):
    for b in range(out_ref.shape[0] // 128):
        row = ids_ref[:, b * 128 : (b + 1) * 128]
        out_ref[b * 128 : (b + 1) * 128, :] = jnp.broadcast_to(row, (128, 128)).T


def positions(first):
    return first + lax.broadcasted_iota(jnp.int32, (BLOCK, 1), 0)


def one_chunk(q, k, qid, kid, bias, keep):
    half = lax.dot_general(q, k, NT, preferred_element_type=jnp.float32)
    same = jnp.concatenate([qid] * (BLOCK // 128), axis=1) == kid
    half = half + jnp.where(same, bias, 0.0)
    weights = half * jnp.tanh(half) + half
    if keep is not None:
        weights = jnp.where(keep, weights, 0.0)
    return weights.astype(jnp.bfloat16)


def own_kernel(meta, bias_ref, x_ref, w_ref, ids_ref, gate_ref, q_ref, part_ref, k_buf, v_buf, qid_buf):
    rows, width = x_ref.shape
    heads = q_ref.shape[0]
    hd = width // heads
    length, start = meta[0], meta[1]
    scale = 0.5 / math.sqrt(hd)
    spread_ids(ids_ref, qid_buf)
    for r in range(rows // BLOCK):
        rs = slice(r * BLOCK, (r + 1) * BLOCK)
        x = x_ref[rs, :]
        gate_ref[rs, :] = silu(mm(x, w_ref[:, :width])).astype(jnp.bfloat16)
        pos = positions(start + r * BLOCK)
        v = jnp.where(pos < length, silu(mm(x, w_ref[:, width : 2 * width])), 0.0).astype(jnp.bfloat16)
        q = silu(mm(x, w_ref[:, 2 * width : 3 * width])).astype(jnp.bfloat16).astype(jnp.float32) * scale
        q = q.astype(jnp.bfloat16)
        k = silu(mm(x, w_ref[:, 3 * width :])).astype(jnp.bfloat16)
        for h in range(heads):
            cs = slice(h * hd, (h + 1) * hd)
            v_buf[h, rs, :] = v[:, cs]
            q_ref[h, rs, :] = q[:, cs]
            k_buf[h, rs, :] = k[:, cs]
    row = lax.broadcasted_iota(jnp.int32, (BLOCK, BLOCK), 0)
    col = lax.broadcasted_iota(jnp.int32, (BLOCK, BLOCK), 1)

    def head(h, carry):
        bias = 0.5 * bias_ref[h]
        for r in range(rows // BLOCK):
            rs = slice(r * BLOCK, (r + 1) * BLOCK)
            q, qid = q_ref[h, rs, :], qid_buf[rs, :]
            acc = None
            for c in range(r + 1):
                cs = slice(c * BLOCK, (c + 1) * BLOCK)
                weights = one_chunk(
                    q, k_buf[h, cs, :], qid, ids_ref[:, cs], bias, col <= row if c == r else None
                )
                term = mm(weights, v_buf[h, cs, :])
                acc = term if acc is None else acc + term
            part_ref[h, rs, :] = acc
        return carry

    lax.fori_loop(0, heads, head, 0)


def halo_kernel(
    meta, bias_ref, x_ref, w_ref, ids_ref, own_ids_ref, events_ref, gate_ref, q_ref, part_ref, w_out_ref,
    out_ref, k_buf, v_buf, qid_buf, mix_buf, gated_buf,
):
    rows, width = x_ref.shape
    heads = q_ref.shape[0]
    hd = width // heads
    length, start = meta[0], meta[1]
    spread_ids(own_ids_ref, qid_buf)
    for r in range(rows // BLOCK):
        rs = slice(r * BLOCK, (r + 1) * BLOCK)
        x = x_ref[rs, :]
        pos = positions(start - WINDOW + r * BLOCK)
        v = silu(mm(x, w_ref[:, width : 2 * width]))
        v = jnp.where((pos >= 0) & (pos < length), v, 0.0).astype(jnp.bfloat16)
        k = silu(mm(x, w_ref[:, 3 * width :])).astype(jnp.bfloat16)
        for h in range(heads):
            cs = slice(h * hd, (h + 1) * hd)
            v_buf[h, rs, :] = v[:, cs]
            k_buf[h, rs, :] = k[:, cs]
    row = lax.broadcasted_iota(jnp.int32, (BLOCK, BLOCK), 0)
    col = lax.broadcasted_iota(jnp.int32, (BLOCK, BLOCK), 1)

    def head(h, carry):
        bias = 0.5 * bias_ref[h]
        for r in range(rows // BLOCK):
            rs = slice(r * BLOCK, (r + 1) * BLOCK)
            q, qid = q_ref[h, rs, :], qid_buf[rs, :]
            acc = part_ref[h, rs, :]
            for c in range(r, rows // BLOCK):
                cs = slice(c * BLOCK, (c + 1) * BLOCK)
                weights = one_chunk(
                    q, k_buf[h, cs, :], qid, ids_ref[:, cs], bias, col > row if c == r else None
                )
                acc = acc + mm(weights, v_buf[h, cs, :])
            mix_buf[h, rs, :] = acc
        return carry

    lax.fori_loop(0, heads, head, 0)
    for r in range(rows // BLOCK):
        rs = slice(r * BLOCK, (r + 1) * BLOCK)
        mixed = jnp.concatenate([mix_buf[h, rs, :] for h in range(heads)], axis=1)
        centered = mixed - jnp.mean(mixed, axis=1, keepdims=True)
        spread = jnp.mean(centered * centered, axis=1, keepdims=True)
        normed = centered * lax.rsqrt(spread + 1e-06 * WINDOW * WINDOW)
        gated_buf[rs, :] = (normed * gate_ref[rs, :].astype(jnp.float32)).astype(jnp.bfloat16)
    place = start + lax.broadcasted_iota(jnp.int32, (8, rows), 1)
    counted = jnp.where(place < length, 1.0, 0.0).astype(jnp.bfloat16)
    gated_sum = mm(counted, gated_buf[...])
    event_sum = mm(counted, events_ref[...])
    projected = jnp.dot(
        gated_sum, w_out_ref[...].astype(jnp.float32),
        preferred_element_type=jnp.float32, precision=lax.Precision.HIGHEST,
    )
    total = (projected + event_sum)[:1]
    for j in range(out_ref.shape[0]):
        out_ref[j] = total


SMEM = pl.BlockSpec(memory_space=pltpu.SMEM)
VMEM = pl.BlockSpec(memory_space=pltpu.VMEM)


def own_part(meta, bias, x, w, ids):
    rows, width = x.shape
    heads = bias.shape[0]
    hd = width // heads
    return pl.pallas_call(
        own_kernel,
        out_shape=(
            jax.ShapeDtypeStruct((rows, width), jnp.bfloat16),
            jax.ShapeDtypeStruct((heads, rows, hd), jnp.bfloat16),
            jax.ShapeDtypeStruct((heads, rows, hd), jnp.float32),
        ),
        in_specs=[SMEM, SMEM, VMEM, VMEM, VMEM],
        out_specs=(VMEM, VMEM, VMEM),
        scratch_shapes=[
            pltpu.VMEM((heads, rows, hd), jnp.bfloat16),
            pltpu.VMEM((heads, rows, hd), jnp.bfloat16),
            pltpu.VMEM((rows, 128), jnp.int32),
        ],
        compiler_params=pltpu.CompilerParams(vmem_limit_bytes=24 << 20),
        cost_estimate=pl.CostEstimate(flops=8 * 10**9, bytes_accessed=10**7, transcendentals=4 * 10**6),
        name="own_part",
    )(meta, bias, x, w, ids)


def halo_part(copies, meta, bias, halo, w, halo_ids, ids, x, gate, q, part, w_out):
    rows, width = x.shape
    heads = bias.shape[0]
    hd = width // heads
    return pl.pallas_call(
        halo_kernel,
        out_shape=jax.ShapeDtypeStruct((copies, 1, width), jnp.float32),
        in_specs=[SMEM, SMEM] + [VMEM] * 9,
        out_specs=VMEM,
        scratch_shapes=[
            pltpu.VMEM((heads, rows, hd), jnp.bfloat16),
            pltpu.VMEM((heads, rows, hd), jnp.bfloat16),
            pltpu.VMEM((rows, 128), jnp.int32),
            pltpu.VMEM((heads, rows, hd), jnp.float32),
            pltpu.VMEM((rows, width), jnp.bfloat16),
        ],
        compiler_params=pltpu.CompilerParams(vmem_limit_bytes=24 << 20),
        name="halo_part",
    )(meta, bias, halo, w, halo_ids, ids, x, gate, q, part, w_out)


def shifted(block, axis, distance):
    devices = range(lax.axis_size(axis))
    route = [(i - distance, i) for i in devices if i - distance in devices]
    return lax.ppermute(block, axis, route)


def local_pool(events, item_ids, lengths, w_proj, w_out, repeat_bias):
    x = events[0]
    start = lax.axis_index("hist") * x.shape[0]
    meta = jnp.stack([lengths[0], start]).astype(jnp.int32)
    halo = shifted(x, "hist", 1)
    halo_ids = shifted(item_ids, "hist", 1)
    gate, q, part = own_part(meta, repeat_bias, x, w_proj, item_ids)
    copies = lax.axis_size("hist")
    return halo_part(
        copies, meta, repeat_bias, halo, w_proj, halo_ids, item_ids, x, gate, q, part, w_out
    )


def vector_kernel(parts_ref, out_ref):
    pooled = parts_ref[0]
    for j in range(1, parts_ref.shape[0]):
        pooled = pooled + parts_ref[j]
    normed = pooled * lax.rsqrt(jnp.mean(pooled * pooled, axis=1, keepdims=True) + 1e-06)
    normed = normed.astype(jnp.bfloat16).astype(jnp.float32)
    for j in range(out_ref.shape[0]):
        out_ref[j] = normed


def as_row(column):
    users = column.shape[0]
    square = jnp.concatenate(
        [jnp.broadcast_to(column, (users, 128)), jnp.zeros((128 - users, 128), jnp.float32)], axis=0
    )
    return square.T[:1]


def logit_kernel(vecs_ref, slab_ref, logits_ref, lse_ref):
    vecs = jnp.concatenate([vecs_ref[j] for j in range(vecs_ref.shape[0])], axis=0).astype(jnp.bfloat16)
    logits = 4.0 * lax.dot_general(vecs, slab_ref[...], NT, preferred_element_type=jnp.float32)
    logits_ref[...] = logits
    top = jnp.max(logits, axis=1, keepdims=True)
    lse = top + jnp.log(jnp.sum(jnp.exp(logits - top), axis=1, keepdims=True))
    row = as_row(lse)
    for j in range(lse_ref.shape[0]):
        lse_ref[j] = row


def joined(parts_ref):
    parts = [parts_ref[j] for j in range(parts_ref.shape[0])]
    top = functools.reduce(jnp.maximum, parts)
    return top + jnp.log(sum(jnp.exp(p - top) for p in parts))


def join_kernel(parts_ref, out_ref):
    lse = joined(parts_ref)
    for j in range(out_ref.shape[0]):
        out_ref[j] = lse


def final_kernel(parts_ref, logits_ref, out_ref):
    users = logits_ref.shape[0]
    lse = jnp.broadcast_to(joined(parts_ref), (128, 128)).T[:users, :1]
    out_ref[...] = logits_ref[...] - lse


def small(kernel, outs, *args, name):
    return pl.pallas_call(
        kernel,
        out_shape=outs,
        in_specs=[VMEM] * len(args),
        out_specs=jax.tree.map(lambda _: VMEM, outs),
        compiler_params=pltpu.CompilerParams(vmem_limit_bytes=16 << 20),
        name=name,
    )(*args)


def swapped(x, axis):
    return lax.all_to_all(x, axis, 0, 0, tiled=True)


def local(events, item_ids, lengths, w_proj, w_out, repeat_bias, item_slab):
    f32 = functools.partial(jax.ShapeDtypeStruct, dtype=jnp.float32)
    hists, items = lax.axis_size("hist"), lax.axis_size("item")
    users, width = items * events.shape[0], events.shape[2]
    parts = local_pool(events, item_ids, lengths, w_proj, w_out, repeat_bias)
    vecs = small(vector_kernel, f32((items, 1, width)), swapped(parts, "hist"), name="vectors")
    logits, lse = small(
        logit_kernel, (f32((users, item_slab.shape[0])), f32((hists, 1, 128))),
        swapped(vecs, "item"), item_slab, name="logits",
    )
    lse = small(join_kernel, f32((items, 1, 128)), swapped(lse, "hist"), name="join")
    return small(final_kernel, f32(logits.shape), swapped(lse, "item"), logits, name="final")


def solution(mesh):
    placed = (
        P("item", "hist", None),
        P("item", "hist"),
        P("item"),
        P(),
        P(),
        P(),
        P(("hist", "item"), None),
    )
    return jax.shard_map(
        local, mesh=mesh, in_specs=placed, out_specs=P(None, ("hist", "item")), check_vma=False
    )
```

```python
import functools
import math

import jax
import jax.numpy as jnp
from jax import lax
from jax.experimental import pallas as pl
from jax.experimental.pallas import tpu as pltpu
from jax.sharding import PartitionSpec as P

WINDOW = 1024
BLOCK = 256
NT = (((1,), (1,)), ((), ()))


def mm(a, b):
    return jnp.dot(a, b, preferred_element_type=jnp.float32)


def silu(x):
    half = 0.5 * x
    return half * jnp.tanh(half) + half


def spread_ids(ids_ref, out_ref):
    for b in range(out_ref.shape[0] // 128):
        row = ids_ref[:, b * 128 : (b + 1) * 128]
        out_ref[b * 128 : (b + 1) * 128, :] = jnp.broadcast_to(row, (128, 128)).T


def weigh(half, qid, kid, bias, keep):
    same = jnp.concatenate([qid] * (half.shape[1] // 128), axis=1) == kid
    half = half + jnp.where(same, bias, 0.0)
    weights = half * jnp.tanh(half) + half
    if keep is not None:
        weights = jnp.where(keep, weights, 0.0)
    return weights.astype(jnp.bfloat16)


def attend(pairs, q_of, k_of, v_of, qid_of, kid_of, bias, keep_of, start_of, store):
    steps = [(r, c) for r, cs in pairs for c in cs]

    def scores(step):
        return lax.dot_general(q_of(step[0]), k_of(step[1]), NT, preferred_element_type=jnp.float32)

    ahead = scores(steps[0])
    done = 0
    for r, cs in pairs:
        acc = start_of(r)
        for c in cs:
            half = ahead
            done += 1
            if done < len(steps):
                ahead = scores(steps[done])
            weights = weigh(half, qid_of(r), kid_of(c), bias, keep_of(r, c))
            term = mm(weights, v_of(c))
            acc = term if acc is None else acc + term
        store(r, acc)


def triangle():
    row = lax.broadcasted_iota(jnp.int32, (BLOCK, BLOCK), 0)
    col = lax.broadcasted_iota(jnp.int32, (BLOCK, BLOCK), 1)
    return col <= row


def part(b):
    return slice(b * BLOCK, (b + 1) * BLOCK)


def own_kernel(
    x_hbm, w_hbm, ids_hbm, bias_hbm, length_ref, gate_ref, q_ref, part_ref,
    x_ref, w_ref, ids_ref, bias_ref, k_buf, v_buf, qid_buf, sems, w_sems,
):
    rows, width = x_ref.shape
    heads = q_ref.shape[0]
    hd = width // heads
    blocks = rows // BLOCK
    cols = w_sems.shape[0]
    start = lax.axis_index("hist") * rows
    fetches = [
        pltpu.make_async_copy(x_hbm.at[0], x_ref, sems.at[0]),
        pltpu.make_async_copy(ids_hbm, ids_ref, sems.at[1]),
        pltpu.make_async_copy(bias_hbm, bias_ref, sems.at[2]),
    ]
    step = w_hbm.shape[1] // cols
    w_fetches = [
        pltpu.make_async_copy(
            w_hbm.at[:, c * step : (c + 1) * step], w_ref.at[:, c * step : (c + 1) * step], w_sems.at[c]
        )
        for c in range(cols)
    ]
    for copy in fetches[:1] + w_fetches + fetches[1:]:
        copy.start()
    fetches[0].wait()
    scale = 0.5 / math.sqrt(hd)
    for c in range(cols):
        w_fetches[c].wait()
        at = c * step
        kind, at = at // width, at % width
        for r in range(0, rows, M):
            rs = slice(r, r + M)
            y = silu(mm(x_ref[rs, :], w_ref[:, c * step : (c + 1) * step]))
            if kind == 0:
                gate_ref[rs, at : at + step] = y
                continue
            if kind == 1:
                pos = start + r + lax.broadcasted_iota(jnp.int32, (M, 1), 0)
                y = jnp.where(pos < length_ref[0], y, 0.0)
            if kind == 2:
                y = y.astype(jnp.bfloat16).astype(jnp.float32) * scale
            y = y.astype(jnp.bfloat16)
            buf = (None, v_buf, q_ref, k_buf)[kind]
            for h in range(step // hd):
                buf[at // hd + h, rs, :] = y[:, h * hd : (h + 1) * hd]
    for copy in fetches[1:]:
        copy.wait()
    spread_ids(ids_ref, qid_buf)
    keep = triangle()

    def head(h, carry):
        def store(r, acc):
            part_ref[h, part(r), :] = acc

        attend(
            [(r, range(r + 1)) for r in range(blocks)],
            lambda r: q_ref[h, part(r), :], lambda c: k_buf[h, part(c), :], lambda c: v_buf[h, part(c), :],
            lambda r: qid_buf[part(r), :], lambda c: ids_ref[:, part(c)], 0.5 * bias_ref[h],
            lambda r, c: keep if r == c else None, lambda r: None, store,
        )
        return carry

    lax.fori_loop(0, heads, head, 0)


def halo_kernel(
    length_ref, bias_ref, x_ref, w_ref, ids_ref, own_ids_ref, events_ref, gate_ref, q_ref, part_ref, w_out_ref,
    out_ref, k_buf, v_buf, qid_buf, mix_buf, gated_buf,
):
    rows, width = x_ref.shape
    heads = q_ref.shape[0]
    hd = width // heads
    blocks = rows // BLOCK
    length, start = length_ref[0], lax.axis_index("hist") * rows
    spread_ids(own_ids_ref, qid_buf)
    step = 256
    for kind, buf in ((1, v_buf), (3, k_buf)):
        for at in range(0, width, step):
            for r in range(0, rows, M):
                rs = slice(r, r + M)
                y = silu(mm(x_ref[rs, :], w_ref[:, kind * width + at : kind * width + at + step]))
                if kind == 1:
                    pos = start - WINDOW + r + lax.broadcasted_iota(jnp.int32, (M, 1), 0)
                    y = jnp.where((pos >= 0) & (pos < length), y, 0.0)
                y = y.astype(jnp.bfloat16)
                for h in range(step // hd):
                    buf[at // hd + h, rs, :] = y[:, h * hd : (h + 1) * hd]
    keep = jnp.logical_not(triangle())

    def head(h, carry):
        def store(r, acc):
            mix_buf[h, part(r), :] = acc

        attend(
            [(r, range(r, blocks)) for r in range(blocks)],
            lambda r: q_ref[h, part(r), :], lambda c: k_buf[h, part(c), :], lambda c: v_buf[h, part(c), :],
            lambda r: qid_buf[part(r), :], lambda c: ids_ref[:, part(c)], 0.5 * bias_ref[h],
            lambda r, c: keep if r == c else None, lambda r: part_ref[h, part(r), :], store,
        )
        return carry

    lax.fori_loop(0, heads, head, 0)

    def norm_rows(b, carry):
        rs = pl.ds(pl.multiple_of(b * NORM_ROWS, NORM_ROWS), NORM_ROWS)
        mixed = [mix_buf[h, rs, :] for h in range(heads)]
        mean = jnp.sum(sum(mixed), axis=1, keepdims=True) * (1.0 / width)
        mixed = [m - mean for m in mixed]
        spread = jnp.sum(sum(m * m for m in mixed), axis=1, keepdims=True) * (1.0 / width)
        factor = lax.rsqrt(spread + 1e-06 * WINDOW * WINDOW)
        for h in range(heads):
            gated = mixed[h] * factor * gate_ref[rs, h * hd : (h + 1) * hd]
            gated_buf[rs, h * hd : (h + 1) * hd] = gated.astype(jnp.bfloat16)
        return carry

    lax.fori_loop(0, rows // NORM_ROWS, norm_rows, 0, unroll=NORM_UNROLL)
    place = start + lax.broadcasted_iota(jnp.int32, (8, rows), 1)
    counted = jnp.where(place < length, 1.0, 0.0).astype(jnp.bfloat16)
    gated_sum = mm(counted, gated_buf[...])
    event_sum = mm(counted, events_ref[...])
    projected = jnp.dot(
        gated_sum, w_out_ref[...].astype(jnp.float32),
        preferred_element_type=jnp.float32, precision=lax.Precision.HIGHEST,
    )
    total = (projected + event_sum)[:1]
    for j in range(out_ref.shape[0]):
        out_ref[j] = total


M = 512
NORM_ROWS = 32
NORM_UNROLL = 4
SMEM = pl.BlockSpec(memory_space=pltpu.SMEM)
VMEM = pl.BlockSpec(memory_space=pltpu.VMEM)


HBM = pl.BlockSpec(memory_space=pltpu.MemorySpace.HBM)


def own_part(events, w, ids, length, bias):
    _, rows, width = events.shape
    heads = bias.shape[0]
    hd = width // heads
    cols = 4
    return pl.pallas_call(
        own_kernel,
        out_shape=(
            jax.ShapeDtypeStruct((rows, width), jnp.float32),
            jax.ShapeDtypeStruct((heads, rows, hd), jnp.bfloat16),
            jax.ShapeDtypeStruct((heads, rows, hd), jnp.float32),
        ),
        in_specs=[HBM] * 4 + [SMEM],
        out_specs=(VMEM, VMEM, VMEM),
        scratch_shapes=[
            pltpu.VMEM((rows, width), jnp.bfloat16),
            pltpu.VMEM(w.shape, jnp.bfloat16),
            pltpu.VMEM(ids.shape, jnp.int32),
            pltpu.SMEM(bias.shape, jnp.float32),
            pltpu.VMEM((heads, rows, hd), jnp.bfloat16),
            pltpu.VMEM((heads, rows, hd), jnp.bfloat16),
            pltpu.VMEM((rows, 128), jnp.int32),
            pltpu.SemaphoreType.DMA((3,)),
            pltpu.SemaphoreType.DMA((cols,)),
        ],
        compiler_params=pltpu.CompilerParams(vmem_limit_bytes=26 << 20),
        cost_estimate=pl.CostEstimate(flops=8 * 10**9, bytes_accessed=10**7, transcendentals=4 * 10**6),
        name="own_part",
    )(*[pltpu.with_memory_space_constraint(a, pltpu.MemorySpace.HBM) for a in (events, w, ids, bias)], length)


def halo_part(copies, length, bias, halo, w, halo_ids, ids, x, gate, q, part, w_out):
    rows, width = x.shape
    heads = bias.shape[0]
    hd = width // heads
    return pl.pallas_call(
        halo_kernel,
        out_shape=jax.ShapeDtypeStruct((copies, 1, width), jnp.float32),
        in_specs=[SMEM, SMEM] + [VMEM] * 9,
        out_specs=VMEM,
        scratch_shapes=[
            pltpu.VMEM((heads, rows, hd), jnp.bfloat16),
            pltpu.VMEM((heads, rows, hd), jnp.bfloat16),
            pltpu.VMEM((rows, 128), jnp.int32),
            pltpu.VMEM((heads, rows, hd), jnp.float32),
            pltpu.VMEM((rows, width), jnp.bfloat16),
        ],
        compiler_params=pltpu.CompilerParams(vmem_limit_bytes=24 << 20),
        name="halo_part",
    )(length, bias, halo, w, halo_ids, ids, x, gate, q, part, w_out)


def shifted(block, axis, distance):
    devices = range(lax.axis_size(axis))
    route = [(i - distance, i) for i in devices if i - distance in devices]
    return lax.ppermute(block, axis, route)


def local_pool(events, item_ids, lengths, w_proj, w_out, repeat_bias):
    x = events[0]
    halo = shifted(x, "hist", 1)
    halo_ids = shifted(item_ids, "hist", 1)
    gate, q, part = own_part(events, w_proj, item_ids, lengths, repeat_bias)
    copies = lax.axis_size("hist")
    return halo_part(
        copies, lengths, repeat_bias, halo, w_proj, halo_ids, item_ids, x, gate, q, part, w_out
    )


def vector_kernel(parts_ref, out_ref):
    pooled = parts_ref[0]
    for j in range(1, parts_ref.shape[0]):
        pooled = pooled + parts_ref[j]
    normed = pooled * lax.rsqrt(jnp.mean(pooled * pooled, axis=1, keepdims=True) + 1e-06)
    normed = normed.astype(jnp.bfloat16).astype(jnp.float32)
    for j in range(out_ref.shape[0]):
        out_ref[j] = normed


def as_row(column):
    users = column.shape[0]
    square = jnp.concatenate(
        [jnp.broadcast_to(column, (users, 128)), jnp.zeros((128 - users, 128), jnp.float32)], axis=0
    )
    return square.T[:1]


def logit_kernel(vecs_ref, slab_ref, logits_ref, lse_ref):
    vecs = jnp.concatenate([vecs_ref[j] for j in range(vecs_ref.shape[0])], axis=0).astype(jnp.bfloat16)
    logits = 4.0 * lax.dot_general(vecs, slab_ref[...], NT, preferred_element_type=jnp.float32)
    logits_ref[...] = logits
    top = jnp.max(logits, axis=1, keepdims=True)
    lse = top + jnp.log(jnp.sum(jnp.exp(logits - top), axis=1, keepdims=True))
    row = as_row(lse)
    for j in range(lse_ref.shape[0]):
        lse_ref[j] = row


def joined(parts_ref):
    parts = [parts_ref[j] for j in range(parts_ref.shape[0])]
    top = functools.reduce(jnp.maximum, parts)
    return top + jnp.log(sum(jnp.exp(p - top) for p in parts))


def join_kernel(parts_ref, out_ref):
    lse = joined(parts_ref)
    for j in range(out_ref.shape[0]):
        out_ref[j] = lse


def final_kernel(parts_ref, logits_ref, out_ref):
    users = logits_ref.shape[0]
    lse = jnp.broadcast_to(joined(parts_ref), (128, 128)).T[:users, :1]
    out_ref[...] = logits_ref[...] - lse


def small(kernel, outs, *args, name):
    return pl.pallas_call(
        kernel,
        out_shape=outs,
        in_specs=[VMEM] * len(args),
        out_specs=jax.tree.map(lambda _: VMEM, outs),
        compiler_params=pltpu.CompilerParams(vmem_limit_bytes=16 << 20),
        name=name,
    )(*args)


def swapped(x, axis):
    return lax.all_to_all(x, axis, 0, 0, tiled=True)


def local(events, item_ids, lengths, w_proj, w_out, repeat_bias, item_slab):
    f32 = functools.partial(jax.ShapeDtypeStruct, dtype=jnp.float32)
    hists, items = lax.axis_size("hist"), lax.axis_size("item")
    users, width = items * events.shape[0], events.shape[2]
    parts = local_pool(events, item_ids, lengths, w_proj, w_out, repeat_bias)
    vecs = small(vector_kernel, f32((items, 1, width)), swapped(parts, "hist"), name="vectors")
    logits, lse = small(
        logit_kernel, (f32((users, item_slab.shape[0])), f32((hists, 1, 128))),
        swapped(vecs, "item"), item_slab, name="logits",
    )
    lse = small(join_kernel, f32((items, 1, 128)), swapped(lse, "hist"), name="join")
    return small(final_kernel, f32(logits.shape), swapped(lse, "item"), logits, name="final")


def solution(mesh):
    placed = (
        P("item", "hist", None),
        P("item", "hist"),
        P("item"),
        P(),
        P(),
        P(),
        P(("hist", "item"), None),
    )
    return jax.shard_map(
        local, mesh=mesh, in_specs=placed, out_specs=P(None, ("hist", "item")), check_vma=False
    )
```

```python
import functools
import math

import jax
import jax.numpy as jnp
from jax import lax
from jax.experimental import pallas as pl
from jax.experimental.pallas import tpu as pltpu
from jax.sharding import PartitionSpec as P

WINDOW = 1024
BLOCK = 256
NT = (((1,), (1,)), ((), ()))


def mm(a, b):
    return jnp.dot(a, b, preferred_element_type=jnp.float32)


def silu(x):
    half = 0.5 * x
    return half * jnp.tanh(half) + half


def spread_ids(ids_ref, out_ref):
    for b in range(out_ref.shape[0] // 128):
        row = ids_ref[:, b * 128 : (b + 1) * 128]
        out_ref[b * 128 : (b + 1) * 128, :] = jnp.broadcast_to(row, (128, 128)).T


def part(b):
    return slice(b * BLOCK, (b + 1) * BLOCK)


def mark_same(row_ids_ref, col_ids_ref, spread, out_ref, row_blocks):
    spread_ids(row_ids_ref, spread)
    for c, rows in enumerate(row_blocks):
        for r in rows:
            mine = jnp.concatenate([spread[part(r), :]] * (BLOCK // 128), axis=1)
            same = mine == col_ids_ref[:, part(c)]
            out_ref[part(r), part(c)] = jnp.where(same, 1.0, 0.0)


def weigh(half, same, bias):
    half = half + same * bias
    return (half * jnp.tanh(half) + half).astype(jnp.bfloat16)


def columns(x_ref, w_ref, first, count, step, emit):
    for at in range(first, first + count, step):
        half = mm(x_ref[...], w_ref[:, at : at + step])
        emit(at, half * jnp.tanh(half) + half)


def put_heads(buf, at, y, hd):
    y = y.astype(jnp.bfloat16)
    for h in range(y.shape[1] // hd):
        buf[at // hd + h] = y[:, h * hd : (h + 1) * hd]


def own_kernel(
    x_hbm, w_hbm, ids_hbm, bias_hbm, length_ref, gate_ref, q_ref, part_ref,
    x_ref, w_ref, ids_ref, bias_ref, k_buf, v_buf, spread, same_buf, tri_buf, sems, w_sems,
):
    rows, width = x_ref.shape
    heads = q_ref.shape[0]
    hd = width // heads
    blocks = rows // BLOCK
    start = lax.axis_index("hist") * rows
    fetch_x = pltpu.make_async_copy(x_hbm.at[0], x_ref, sems.at[0])
    fetch_ids = pltpu.make_async_copy(ids_hbm, ids_ref, sems.at[1])
    fetch_bias = pltpu.make_async_copy(bias_hbm, bias_ref, sems.at[2])
    cut = 2 * width
    fetch_w = [
        pltpu.make_async_copy(
            w_hbm.at[:, i * cut : (i + 1) * cut], w_ref.at[:, i * cut : (i + 1) * cut], w_sems.at[i]
        )
        for i in range(2)
    ]
    for copy in (fetch_ids, fetch_bias, fetch_x, *fetch_w):
        copy.start()
    row = lax.broadcasted_iota(jnp.int32, (BLOCK, BLOCK), 0)
    col = lax.broadcasted_iota(jnp.int32, (BLOCK, BLOCK), 1)
    tri_buf[...] = jnp.where(col <= row, 1.0, 0.0).astype(jnp.bfloat16)
    fetch_ids.wait()
    fetch_bias.wait()
    mark_same(ids_ref, ids_ref, spread, same_buf, [range(c, blocks) for c in range(blocks)])
    fetch_x.wait()
    x_ref[...] = x_ref[...] * jnp.bfloat16(0.5)

    def emit(at, y):
        kind, at = at // width, at % width
        if kind == 0:
            gate_ref[:, at : at + y.shape[1]] = y
        elif kind == 1:
            pos = start + lax.broadcasted_iota(jnp.int32, (rows, 1), 0)
            put_heads(v_buf, at, jnp.where(pos < length_ref[0], y, 0.0), hd)
        elif kind == 2:
            put_heads(q_ref, at, y * (0.5 / math.sqrt(hd)), hd)
        else:
            put_heads(k_buf, at, y, hd)

    for i in range(2):
        fetch_w[i].wait()
        columns(x_ref, w_ref, i * cut, cut, 256, emit)
    for h in range(heads):
        bias = 0.5 * bias_ref[h]
        for c in range(blocks):
            rs = slice(c * BLOCK, rows)
            half = lax.dot_general(q_ref[h, rs, :], k_buf[h, part(c), :], NT, preferred_element_type=jnp.float32)
            weights = weigh(half, same_buf[rs, part(c)], bias)
            edge = weights[:BLOCK] * tri_buf[...]
            if c < blocks - 1:
                edge = jnp.concatenate([edge, weights[BLOCK:]], axis=0)
            term = mm(edge, v_buf[h, part(c), :])
            part_ref[h, rs, :] = term if c == 0 else part_ref[h, rs, :] + term


def halo_kernel(
    length_ref, bias_ref, halo_ref, w_ref, ids_ref, own_ids_ref, events_ref, gate_ref, q_ref, part_ref, w_out_ref,
    out_ref, x_ref, k_buf, v_buf, spread, same_buf, tri_buf, mix_buf, gated_buf,
):
    rows, width = x_ref.shape
    heads = q_ref.shape[0]
    hd = width // heads
    blocks = rows // BLOCK
    length, start = length_ref[0], lax.axis_index("hist") * rows
    row = lax.broadcasted_iota(jnp.int32, (BLOCK, BLOCK), 0)
    col = lax.broadcasted_iota(jnp.int32, (BLOCK, BLOCK), 1)
    tri_buf[...] = jnp.where(col > row, 1.0, 0.0).astype(jnp.bfloat16)
    x_ref[...] = halo_ref[...] * jnp.bfloat16(0.5)
    mark_same(own_ids_ref, ids_ref, spread, same_buf, [range(c + 1) for c in range(blocks)])

    def emit(at, y):
        kind, at = at // width, at % width
        if kind == 1:
            pos = start - WINDOW + lax.broadcasted_iota(jnp.int32, (rows, 1), 0)
            put_heads(v_buf, at, jnp.where((pos >= 0) & (pos < length), y, 0.0), hd)
        else:
            put_heads(k_buf, at, y, hd)

    columns(x_ref, w_ref, width, width, 256, emit)
    columns(x_ref, w_ref, 3 * width, width, 256, emit)
    for h in range(heads):
        bias = 0.5 * bias_ref[h]
        for c in range(blocks - 1, -1, -1):
            rs = slice(0, (c + 1) * BLOCK)
            half = lax.dot_general(q_ref[h, rs, :], k_buf[h, part(c), :], NT, preferred_element_type=jnp.float32)
            weights = weigh(half, same_buf[rs, part(c)], bias)
            edge = weights[c * BLOCK :] * tri_buf[...]
            if c:
                edge = jnp.concatenate([weights[: c * BLOCK], edge], axis=0)
            term = mm(edge, v_buf[h, part(c), :])
            mix_buf[h, rs, :] = (part_ref if c == blocks - 1 else mix_buf)[h, rs, :] + term

    def norm_rows(b, carry):
        rs = pl.ds(pl.multiple_of(b * NORM_ROWS, NORM_ROWS), NORM_ROWS)
        mixed = [mix_buf[h, rs, :] for h in range(heads)]
        mean = jnp.sum(sum(mixed), axis=1, keepdims=True) * (1.0 / width)
        mixed = [m - mean for m in mixed]
        spread = jnp.sum(sum(m * m for m in mixed), axis=1, keepdims=True) * (1.0 / width)
        factor = lax.rsqrt(spread + 1e-06 * WINDOW * WINDOW)
        for h in range(heads):
            gated = mixed[h] * factor * gate_ref[rs, h * hd : (h + 1) * hd]
            gated_buf[rs, h * hd : (h + 1) * hd] = gated.astype(jnp.bfloat16)
        return carry

    lax.fori_loop(0, rows // NORM_ROWS, norm_rows, 0, unroll=NORM_UNROLL)
    place = start + lax.broadcasted_iota(jnp.int32, (8, rows), 1)
    counted = jnp.where(place < length, 1.0, 0.0).astype(jnp.bfloat16)
    gated_sum = mm(counted, gated_buf[...])
    event_sum = mm(counted, events_ref[...])
    high = gated_sum.astype(jnp.bfloat16).astype(jnp.float32)
    middle = (gated_sum - high).astype(jnp.bfloat16).astype(jnp.float32)
    low = gated_sum - high - middle
    which = lax.broadcasted_iota(jnp.int32, gated_sum.shape, 0)
    terms = jnp.where(which == 0, high, jnp.where(which == 1, middle, jnp.where(which == 2, low, 0.0)))
    projected = jnp.sum(mm(terms.astype(jnp.bfloat16), w_out_ref[...]), axis=0, keepdims=True)
    total = projected + event_sum[:1]
    for j in range(out_ref.shape[0]):
        out_ref[j] = total


NORM_ROWS = 32
NORM_UNROLL = 4
SMEM = pl.BlockSpec(memory_space=pltpu.SMEM)
VMEM = pl.BlockSpec(memory_space=pltpu.VMEM)


HBM = pl.BlockSpec(memory_space=pltpu.MemorySpace.HBM)


def own_part(events, w, ids, length, bias):
    _, rows, width = events.shape
    heads = bias.shape[0]
    hd = width // heads
    return pl.pallas_call(
        own_kernel,
        out_shape=(
            jax.ShapeDtypeStruct((rows, width), jnp.float32),
            jax.ShapeDtypeStruct((heads, rows, hd), jnp.bfloat16),
            jax.ShapeDtypeStruct((heads, rows, hd), jnp.float32),
        ),
        in_specs=[HBM] * 4 + [SMEM],
        out_specs=(VMEM, VMEM, VMEM),
        scratch_shapes=[
            pltpu.VMEM((rows, width), jnp.bfloat16),
            pltpu.VMEM(w.shape, jnp.bfloat16),
            pltpu.VMEM(ids.shape, jnp.int32),
            pltpu.SMEM(bias.shape, jnp.float32),
            pltpu.VMEM((heads, rows, hd), jnp.bfloat16),
            pltpu.VMEM((heads, rows, hd), jnp.bfloat16),
            pltpu.VMEM((rows, 128), jnp.int32),
            pltpu.VMEM((rows, rows), jnp.float32),
            pltpu.VMEM((BLOCK, BLOCK), jnp.bfloat16),
            pltpu.SemaphoreType.DMA((3,)),
            pltpu.SemaphoreType.DMA((2,)),
        ],
        compiler_params=pltpu.CompilerParams(vmem_limit_bytes=26 << 20),
        cost_estimate=pl.CostEstimate(flops=8 * 10**9, bytes_accessed=10**7, transcendentals=4 * 10**6),
        name="own_part",
    )(*[pltpu.with_memory_space_constraint(a, pltpu.MemorySpace.HBM) for a in (events, w, ids, bias)], length)


def halo_part(copies, length, bias, halo, w, halo_ids, ids, x, gate, q, part, w_out):
    rows, width = x.shape
    heads = bias.shape[0]
    hd = width // heads
    return pl.pallas_call(
        halo_kernel,
        out_shape=jax.ShapeDtypeStruct((copies, 1, width), jnp.float32),
        in_specs=[SMEM, SMEM] + [VMEM] * 9,
        out_specs=VMEM,
        scratch_shapes=[
            pltpu.VMEM((rows, width), jnp.bfloat16),
            pltpu.VMEM((heads, rows, hd), jnp.bfloat16),
            pltpu.VMEM((heads, rows, hd), jnp.bfloat16),
            pltpu.VMEM((rows, 128), jnp.int32),
            pltpu.VMEM((rows, rows), jnp.float32),
            pltpu.VMEM((BLOCK, BLOCK), jnp.bfloat16),
            pltpu.VMEM((heads, rows, hd), jnp.float32),
            pltpu.VMEM((rows, width), jnp.bfloat16),
        ],
        compiler_params=pltpu.CompilerParams(vmem_limit_bytes=24 << 20),
        name="halo_part",
    )(length, bias, halo, w, halo_ids, ids, x, gate, q, part, w_out)


def shifted(block, axis, distance):
    devices = range(lax.axis_size(axis))
    route = [(i - distance, i) for i in devices if i - distance in devices]
    return lax.ppermute(block, axis, route)


def local_pool(events, item_ids, lengths, w_proj, w_out, repeat_bias):
    x = events[0]
    halo = shifted(x, "hist", 1)
    halo_ids = shifted(item_ids, "hist", 1)
    gate, q, part = own_part(events, w_proj, item_ids, lengths, repeat_bias)
    copies = lax.axis_size("hist")
    return halo_part(
        copies, lengths, repeat_bias, halo, w_proj, halo_ids, item_ids, x, gate, q, part, w_out
    )


def vector_kernel(parts_ref, out_ref):
    pooled = parts_ref[0]
    for j in range(1, parts_ref.shape[0]):
        pooled = pooled + parts_ref[j]
    normed = pooled * lax.rsqrt(jnp.mean(pooled * pooled, axis=1, keepdims=True) + 1e-06)
    normed = normed.astype(jnp.bfloat16).astype(jnp.float32)
    for j in range(out_ref.shape[0]):
        out_ref[j] = normed


def as_row(column):
    users = column.shape[0]
    square = jnp.concatenate(
        [jnp.broadcast_to(column, (users, 128)), jnp.zeros((128 - users, 128), jnp.float32)], axis=0
    )
    return square.T[:1]


def logit_kernel(vecs_ref, slab_ref, logits_ref, lse_ref):
    vecs = jnp.concatenate([vecs_ref[j] for j in range(vecs_ref.shape[0])], axis=0).astype(jnp.bfloat16)
    logits = 4.0 * lax.dot_general(vecs, slab_ref[...], NT, preferred_element_type=jnp.float32)
    logits_ref[...] = logits
    top = jnp.max(logits, axis=1, keepdims=True)
    lse = top + jnp.log(jnp.sum(jnp.exp(logits - top), axis=1, keepdims=True))
    row = as_row(lse)
    for j in range(lse_ref.shape[0]):
        lse_ref[j] = row


def joined(parts_ref):
    parts = [parts_ref[j] for j in range(parts_ref.shape[0])]
    top = functools.reduce(jnp.maximum, parts)
    return top + jnp.log(sum(jnp.exp(p - top) for p in parts))


def join_kernel(parts_ref, out_ref):
    lse = joined(parts_ref)
    for j in range(out_ref.shape[0]):
        out_ref[j] = lse


def final_kernel(parts_ref, logits_ref, out_ref):
    users = logits_ref.shape[0]
    lse = jnp.broadcast_to(joined(parts_ref), (128, 128)).T[:users, :1]
    out_ref[...] = logits_ref[...] - lse


def small(kernel, outs, *args, name):
    return pl.pallas_call(
        kernel,
        out_shape=outs,
        in_specs=[VMEM] * len(args),
        out_specs=jax.tree.map(lambda _: VMEM, outs),
        compiler_params=pltpu.CompilerParams(vmem_limit_bytes=16 << 20),
        name=name,
    )(*args)


def swapped(x, axis):
    return lax.all_to_all(x, axis, 0, 0, tiled=True)


def local(events, item_ids, lengths, w_proj, w_out, repeat_bias, item_slab):
    f32 = functools.partial(jax.ShapeDtypeStruct, dtype=jnp.float32)
    hists, items = lax.axis_size("hist"), lax.axis_size("item")
    users, width = items * events.shape[0], events.shape[2]
    parts = local_pool(events, item_ids, lengths, w_proj, w_out, repeat_bias)
    vecs = small(vector_kernel, f32((items, 1, width)), swapped(parts, "hist"), name="vectors")
    logits, lse = small(
        logit_kernel, (f32((users, item_slab.shape[0])), f32((hists, 1, 128))),
        swapped(vecs, "item"), item_slab, name="logits",
    )
    lse = small(join_kernel, f32((items, 1, 128)), swapped(lse, "hist"), name="join")
    return small(final_kernel, f32(logits.shape), swapped(lse, "item"), logits, name="final")


def solution(mesh):
    placed = (
        P("item", "hist", None),
        P("item", "hist"),
        P("item"),
        P(),
        P(),
        P(),
        P(("hist", "item"), None),
    )
    return jax.shard_map(
        local, mesh=mesh, in_specs=placed, out_specs=P(None, ("hist", "item")), check_vma=False
    )
```

```python
import functools
import math

import jax
import jax.numpy as jnp
from jax import lax
from jax.experimental import pallas as pl
from jax.experimental.pallas import tpu as pltpu
from jax.sharding import PartitionSpec as P


WINDOW = 1024
BLOCK = 256
NT = (((1,), (1,)), ((), ()))


def mm(a, b):
    return jnp.dot(a, b, preferred_element_type=jnp.float32)


def spread_ids(row, out_ref):
    for b in range(out_ref.shape[0] // 128):
        out_ref[b * 128 : (b + 1) * 128, :] = jnp.broadcast_to(row[:, b * 128 : (b + 1) * 128], (128, 128)).T


def part(b):
    return slice(b * BLOCK, (b + 1) * BLOCK)


def mark_same(spread, rows, ids):
    mine = jnp.concatenate([spread[rows, :]] * (ids.shape[1] // 128), axis=1)
    return jnp.where(mine == ids, 1.0, 0.0)


def triangle(below):
    row = lax.broadcasted_iota(jnp.int32, (BLOCK, BLOCK), 0)
    col = lax.broadcasted_iota(jnp.int32, (BLOCK, BLOCK), 1)
    return jnp.where((col <= row) if below else (col > row), 1.0, 0.0).astype(jnp.bfloat16)


def mixed_term(q, k, v, same, bias, tri, at):
    half = lax.dot_general(q, k, NT, preferred_element_type=jnp.float32) + same * bias
    weights = (half * jnp.tanh(half) + half).astype(jnp.bfloat16)
    pieces = [weights[:at], weights[at : at + BLOCK] * tri, weights[at + BLOCK :]]
    pieces = [p for p in pieces if p.shape[0]]
    return mm(jnp.concatenate(pieces, axis=0) if len(pieces) > 1 else pieces[0], v)


def columns(x_ref, w_ref, first, count, emit, base=0):
    for at in range(first, first + count, 256):
        half = mm(x_ref[...], w_ref[:, at - base : at - base + 256])
        emit(at, half * jnp.tanh(half) + half)


def put_heads(buf, at, y, hd):
    y = y.astype(jnp.bfloat16)
    for h in range(y.shape[1] // hd):
        buf[at // hd + h] = y[:, h * hd : (h + 1) * hd]


def digit_rows(ids):
    which = lax.broadcasted_iota(jnp.int32, (16, ids.shape[1]), 0)
    digits = jnp.where(which == 0, ids & 127, jnp.where(which == 1, (ids >> 7) & 127, ids >> 14))
    return jnp.where(which < 3, digits, 0).astype(jnp.float32).astype(jnp.bfloat16)


def from_digits(rows):
    rows = rows.astype(jnp.float32)
    return (rows[0:1] + 128.0 * rows[1:2] + 16384.0 * rows[2:3]).astype(jnp.int32)


def start_kernel(
    x_hbm, w_hbm, ids_hbm, length_ref, high_ref, low_ref, x_ref, gate_ref, v_ref, spread_ref, events_ref,
    w_ref, ids_ref, sems,
):
    rows, width = x_ref.shape
    hd = v_ref.shape[2]
    cut = rows // 2
    start = lax.axis_index("hist") * rows
    copies = [
        pltpu.make_async_copy(ids_hbm, ids_ref, sems.at[0]),
        pltpu.make_async_copy(x_hbm.at[0], events_ref, sems.at[1]),
        pltpu.make_async_copy(w_hbm.at[:, : 2 * width], w_ref, sems.at[2]),
    ]
    for copy in copies:
        copy.start()
    copies[0].wait()
    ids = ids_ref[...]
    spread_ids(ids, spread_ref)
    low_ref[cut:, :] = digit_rows(ids[:, :cut])
    high_ref[cut:, :] = digit_rows(ids[:, cut:])
    copies[1].wait()
    low_ref[:cut, :] = events_ref[:cut, :]
    high_ref[:cut, :] = events_ref[cut:, :]
    x_ref[...] = events_ref[...] * jnp.bfloat16(0.5)
    copies[2].wait()

    def emit(at, y):
        if at < width:
            gate_ref[:, at : at + y.shape[1]] = y
        else:
            pos = start + lax.broadcasted_iota(jnp.int32, (rows, 1), 0)
            put_heads(v_ref, at - width, jnp.where(pos < length_ref[0], y, 0.0), hd)

    columns(x_ref, w_ref, 0, 2 * width, emit)


def own_kernel(bias_ref, x_ref, w_ref, ids_ref, spread_ref, v_ref, q_ref, part_ref, k_buf, same_buf):
    rows, width = x_ref.shape
    heads, _, hd = v_ref.shape
    blocks = rows // BLOCK
    tri = triangle(True)
    for c in range(blocks):
        same_buf[c * BLOCK :, part(c)] = mark_same(spread_ref, slice(c * BLOCK, rows), ids_ref[:, part(c)])

    def emit(at, y):
        if at < 3 * width:
            put_heads(q_ref, at - 2 * width, y * (0.5 / math.sqrt(hd)), hd)
        else:
            put_heads(k_buf, at - 3 * width, y, hd)

    columns(x_ref, w_ref, 2 * width, 2 * width, emit)
    for h in range(heads):
        for c in range(blocks):
            rs = slice(c * BLOCK, rows)
            term = mixed_term(
                q_ref[h, rs, :], k_buf[h, part(c), :], v_ref[h, part(c), :], same_buf[rs, part(c)],
                0.5 * bias_ref[h], tri, 0,
            )
            part_ref[h, rs, :] = term if c == 0 else part_ref[h, rs, :] + term


def halo_piece(first, length, bias_ref, got_ref, w_ref, spread_ref, q_ref, part_ref, x_buf, k_buf, v_buf, same_buf, mix_ref):
    heads, _, hd = q_ref.shape
    keys, width = x_buf.shape
    blocks = keys // BLOCK
    tri = triangle(False)
    x_buf[...] = got_ref[:keys, :] * jnp.bfloat16(0.5)
    ids = from_digits(got_ref[keys:, :])
    for c in range(blocks):
        end = (first + c + 1) * BLOCK
        same_buf[:end, part(c)] = mark_same(spread_ref, slice(0, end), ids[:, part(c)])
    pos = lax.axis_index("hist") * WINDOW - WINDOW + first * BLOCK + lax.broadcasted_iota(jnp.int32, (keys, 1), 0)

    def emit(at, y):
        if at < 2 * width:
            put_heads(v_buf, at - width, jnp.where((pos >= 0) & (pos < length), y, 0.0), hd)
        else:
            put_heads(k_buf, at - 3 * width, y, hd)

    columns(x_buf, w_ref, width, width, emit)
    columns(x_buf, w_ref, 3 * width, width, emit)
    for h in range(heads):
        for c in range(blocks - 1, -1, -1):
            rs = slice(0, (first + c + 1) * BLOCK)
            term = mixed_term(
                q_ref[h, rs, :], k_buf[h, part(c), :], v_buf[h, part(c), :], same_buf[rs, part(c)],
                0.5 * bias_ref[h], tri, (first + c) * BLOCK,
            )
            mix_ref[h, rs, :] = (part_ref if c == blocks - 1 else mix_ref)[h, rs, :] + term


def gated_sum(first, rows, length, mix_ref, gate_ref, gated_buf):
    heads, _, hd = mix_ref.shape
    width = heads * hd

    def norm_rows(b, carry):
        at = pl.multiple_of(b * NORM_ROWS, NORM_ROWS)
        rs = pl.ds(first + at, NORM_ROWS)
        mixed = [mix_ref[h, rs, :] for h in range(heads)]
        mean = jnp.sum(sum(mixed), axis=1, keepdims=True) * (1.0 / width)
        mixed = [m - mean for m in mixed]
        spread = jnp.sum(sum(m * m for m in mixed), axis=1, keepdims=True) * (1.0 / width)
        factor = lax.rsqrt(spread + 1e-06 * WINDOW * WINDOW)
        for h in range(heads):
            gated = mixed[h] * factor * gate_ref[rs, h * hd : (h + 1) * hd]
            gated_buf[pl.ds(at, NORM_ROWS), h * hd : (h + 1) * hd] = gated.astype(jnp.bfloat16)
        return carry

    lax.fori_loop(0, rows // NORM_ROWS, norm_rows, 0, unroll=NORM_UNROLL)
    return mm(valid(first, rows, length), gated_buf[...])


def valid(first, rows, length):
    place = lax.axis_index("hist") * WINDOW + first + lax.broadcasted_iota(jnp.int32, (8, rows), 1)
    return jnp.where(place < length, 1.0, 0.0).astype(jnp.bfloat16)


def high_kernel(
    length_ref, bias_ref, got_ref, w_ref, spread_ref, q_ref, part_ref, gate_ref, events_ref,
    mix_ref, sums_ref, x_buf, k_buf, v_buf, same_buf, gated_buf,
):
    rows = q_ref.shape[1]
    cut = rows // 2
    length = length_ref[0]
    halo_piece(
        cut // BLOCK, length, bias_ref, got_ref, w_ref, spread_ref, q_ref, part_ref, x_buf, k_buf, v_buf, same_buf, mix_ref
    )
    sums_ref[0] = gated_sum(cut, rows - cut, length, mix_ref, gate_ref, gated_buf)
    sums_ref[1] = mm(valid(0, rows, length), events_ref[...])


def low_kernel(
    length_ref, bias_ref, got_ref, w_ref, spread_ref, q_ref, part_ref, gate_ref, sums_ref, w_out_ref,
    out_ref, x_buf, k_buf, v_buf, same_buf, mix_buf, gated_buf,
):
    cut = gated_buf.shape[0]
    length = length_ref[0]
    halo_piece(0, length, bias_ref, got_ref, w_ref, spread_ref, q_ref, part_ref, x_buf, k_buf, v_buf, same_buf, mix_buf)
    total = sums_ref[0] + gated_sum(0, cut, length, mix_buf, gate_ref, gated_buf)
    high = total.astype(jnp.bfloat16).astype(jnp.float32)
    middle = (total - high).astype(jnp.bfloat16).astype(jnp.float32)
    low = total - high - middle
    which = lax.broadcasted_iota(jnp.int32, total.shape, 0)
    terms = jnp.where(which == 0, high, jnp.where(which == 1, middle, jnp.where(which == 2, low, 0.0)))
    projected = jnp.sum(mm(terms.astype(jnp.bfloat16), w_out_ref[...]), axis=0, keepdims=True)
    pooled = projected + sums_ref[1][:1]
    for j in range(out_ref.shape[0]):
        out_ref[j] = pooled


NORM_ROWS = 32
NORM_UNROLL = 4


SMEM = pl.BlockSpec(memory_space=pltpu.SMEM)
VMEM = pl.BlockSpec(memory_space=pltpu.VMEM)


def shifted(block, axis, distance):
    devices = range(lax.axis_size(axis))
    route = [(i - distance, i) for i in devices if i - distance in devices]
    return lax.ppermute(block, axis, route)


HBM = pl.BlockSpec(memory_space=pltpu.MemorySpace.HBM)


def kernel_call(kernel, outs, specs, scratch, args, mflops):
    return pl.pallas_call(
        kernel,
        out_shape=outs,
        in_specs=specs,
        out_specs=jax.tree.map(lambda _: VMEM, outs),
        scratch_shapes=scratch,
        compiler_params=pltpu.CompilerParams(vmem_limit_bytes=24 << 20),
        cost_estimate=pl.CostEstimate(flops=mflops * 10**6, bytes_accessed=10**7, transcendentals=10**6),
    )(*args)


def local_pool(events, item_ids, lengths, w_proj, w_out, repeat_bias):
    _, rows, width = events.shape
    heads = repeat_bias.shape[0]
    hd = width // heads
    cut = rows // 2
    bf16 = functools.partial(jax.ShapeDtypeStruct, dtype=jnp.bfloat16)
    f32 = functools.partial(jax.ShapeDtypeStruct, dtype=jnp.float32)
    stay = [pltpu.with_memory_space_constraint(a, pltpu.MemorySpace.HBM) for a in (events, w_proj, item_ids)]
    high, low, x, gate, v, spread, own = kernel_call(
        start_kernel,
        (
            bf16((cut + 16, width)), bf16((cut + 16, width)), bf16((rows, width)), f32((rows, width)),
            bf16((heads, rows, hd)), jax.ShapeDtypeStruct((rows, 128), jnp.int32), bf16((rows, width)),
        ),
        [HBM] * 3 + [SMEM],
        [
            pltpu.VMEM((width, 2 * width), jnp.bfloat16),
            pltpu.VMEM(item_ids.shape, jnp.int32),
            pltpu.SemaphoreType.DMA((3,)),
        ],
        (*stay, lengths), 1000,
    )
    high = shifted(high, "hist", 1)
    low = shifted(low, "hist", 1)
    q, mixed = kernel_call(
        own_kernel,
        (bf16((heads, rows, hd)), f32((heads, rows, hd))),
        [SMEM] + [VMEM] * 5,
        [pltpu.VMEM((heads, rows, hd), jnp.bfloat16), pltpu.VMEM((rows, rows), jnp.float32)],
        (repeat_bias, x, w_proj, item_ids, spread, v), 6000,
    )
    piece = [
        pltpu.VMEM((cut, width), jnp.bfloat16),
        pltpu.VMEM((heads, cut, hd), jnp.bfloat16),
        pltpu.VMEM((heads, cut, hd), jnp.bfloat16),
    ]
    mixed, sums = kernel_call(
        high_kernel,
        (f32((heads, rows, hd)), f32((2, 8, width))),
        [SMEM] * 2 + [VMEM] * 7,
        piece + [pltpu.VMEM((rows, cut), jnp.float32), pltpu.VMEM((cut, width), jnp.bfloat16)],
        (lengths, repeat_bias, high, w_proj, spread, q, mixed, gate, own), 4000,
    )
    return kernel_call(
        low_kernel,
        f32((lax.axis_size("hist"), 1, width)),
        [SMEM] * 2 + [VMEM] * 8,
        piece + [
            pltpu.VMEM((cut, cut), jnp.float32), pltpu.VMEM((heads, cut, hd), jnp.float32),
            pltpu.VMEM((cut, width), jnp.bfloat16),
        ],
        (lengths, repeat_bias, low, w_proj, spread, q, mixed, gate, sums, w_out), 2000,
    )


def vector_kernel(parts_ref, out_ref):
    pooled = parts_ref[0]
    for j in range(1, parts_ref.shape[0]):
        pooled = pooled + parts_ref[j]
    normed = pooled * lax.rsqrt(jnp.mean(pooled * pooled, axis=1, keepdims=True) + 1e-06)
    normed = normed.astype(jnp.bfloat16).astype(jnp.float32)
    for j in range(out_ref.shape[0]):
        out_ref[j] = normed


def as_row(column):
    users = column.shape[0]
    square = jnp.concatenate(
        [jnp.broadcast_to(column, (users, 128)), jnp.zeros((128 - users, 128), jnp.float32)], axis=0
    )
    return square.T[:1]


def logit_kernel(vecs_ref, slab_ref, logits_ref, lse_ref):
    vecs = jnp.concatenate([vecs_ref[j] for j in range(vecs_ref.shape[0])], axis=0).astype(jnp.bfloat16)
    logits = 4.0 * lax.dot_general(vecs, slab_ref[...], NT, preferred_element_type=jnp.float32)
    logits_ref[...] = logits
    top = jnp.max(logits, axis=1, keepdims=True)
    lse = top + jnp.log(jnp.sum(jnp.exp(logits - top), axis=1, keepdims=True))
    row = as_row(lse)
    for j in range(lse_ref.shape[0]):
        lse_ref[j] = row


def joined(parts_ref):
    parts = [parts_ref[j] for j in range(parts_ref.shape[0])]
    top = functools.reduce(jnp.maximum, parts)
    return top + jnp.log(sum(jnp.exp(p - top) for p in parts))


def join_kernel(parts_ref, out_ref):
    lse = joined(parts_ref)
    for j in range(out_ref.shape[0]):
        out_ref[j] = lse


def final_kernel(parts_ref, logits_ref, out_ref):
    users = logits_ref.shape[0]
    lse = jnp.broadcast_to(joined(parts_ref), (128, 128)).T[:users, :1]
    out_ref[...] = logits_ref[...] - lse


def small(kernel, outs, *args):
    return pl.pallas_call(
        kernel,
        out_shape=outs,
        in_specs=[VMEM] * len(args),
        out_specs=jax.tree.map(lambda _: VMEM, outs),
        compiler_params=pltpu.CompilerParams(vmem_limit_bytes=16 << 20),
    )(*args)


def swapped(x, axis):
    return lax.all_to_all(x, axis, 0, 0, tiled=True)


def local(events, item_ids, lengths, w_proj, w_out, repeat_bias, item_slab):
    f32 = functools.partial(jax.ShapeDtypeStruct, dtype=jnp.float32)
    hists, items = lax.axis_size("hist"), lax.axis_size("item")
    users, width = items * events.shape[0], events.shape[2]
    parts = local_pool(events, item_ids, lengths, w_proj, w_out, repeat_bias)
    vecs = small(vector_kernel, f32((items, 1, width)), swapped(parts, "hist"))
    logits, lse = small(
        logit_kernel, (f32((users, item_slab.shape[0])), f32((hists, 1, 128))),
        swapped(vecs, "item"), item_slab,
    )
    lse = small(join_kernel, f32((items, 1, 128)), swapped(lse, "hist"))
    return small(final_kernel, f32(logits.shape), swapped(lse, "item"), logits)


def solution(mesh):
    placed = (
        P("item", "hist", None),
        P("item", "hist"),
        P("item"),
        P(),
        P(),
        P(),
        P(("hist", "item"), None),
    )
    return jax.shard_map(
        local, mesh=mesh, in_specs=placed, out_specs=P(None, ("hist", "item")), check_vma=False
    )
```

```python
import functools
import math

import jax
import jax.numpy as jnp
from jax import lax
from jax.experimental import pallas as pl
from jax.experimental.pallas import tpu as pltpu
from jax.sharding import PartitionSpec as P


WINDOW = 1024
BLOCK = 256
NT = (((1,), (1,)), ((), ()))


def mm(a, b):
    return jnp.dot(a, b, preferred_element_type=jnp.float32)


def spread_ids(row, out_ref):
    for b in range(out_ref.shape[0] // 128):
        out_ref[b * 128 : (b + 1) * 128, :] = jnp.broadcast_to(row[:, b * 128 : (b + 1) * 128], (128, 128)).T


def part(b):
    return slice(b * BLOCK, (b + 1) * BLOCK)


def mark_same(spread, rows, ids):
    mine = jnp.concatenate([spread[rows, :]] * (ids.shape[1] // 128), axis=1)
    return jnp.where(mine == ids, 1.0, 0.0)


def triangle(below):
    row = lax.broadcasted_iota(jnp.int32, (BLOCK, BLOCK), 0)
    col = lax.broadcasted_iota(jnp.int32, (BLOCK, BLOCK), 1)
    return jnp.where((col <= row) if below else (col > row), 1.0, 0.0).astype(jnp.bfloat16)


def mixed_term(q, k, v, same, bias, tri, at):
    half = lax.dot_general(q, k, NT, preferred_element_type=jnp.float32) + same * bias
    weights = (half * jnp.tanh(half) + half).astype(jnp.bfloat16)
    pieces = [weights[:at], weights[at : at + BLOCK] * tri, weights[at + BLOCK :]]
    pieces = [p for p in pieces if p.shape[0]]
    return mm(jnp.concatenate(pieces, axis=0) if len(pieces) > 1 else pieces[0], v)


def columns(x_ref, w_ref, first, count, emit):
    for at in range(first, first + count, 256):
        half = mm(x_ref[...], w_ref[:, at : at + 256])
        emit(at, half * jnp.tanh(half) + half)


def put_heads(buf, at, y, hd):
    y = y.astype(jnp.bfloat16)
    for h in range(y.shape[1] // hd):
        buf[at // hd + h] = y[:, h * hd : (h + 1) * hd]


def digit_rows(ids):
    which = lax.broadcasted_iota(jnp.int32, (16, ids.shape[1]), 0)
    digits = jnp.where(which == 0, ids & 127, jnp.where(which == 1, (ids >> 7) & 127, ids >> 14))
    return jnp.where(which < 3, digits, 0).astype(jnp.float32).astype(jnp.bfloat16)


def from_digits(rows):
    rows = rows.astype(jnp.float32)
    return (rows[0:1] + 128.0 * rows[1:2] + 16384.0 * rows[2:3]).astype(jnp.int32)


def send_kernel(x_hbm, ids_hbm, high_ref, low_ref, events_ref, ids_ref, sems):
    cut = ids_ref.shape[1] // 2
    copies = [
        pltpu.make_async_copy(x_hbm.at[0, cut:], events_ref.at[cut:], sems.at[0]),
        pltpu.make_async_copy(x_hbm.at[0, :cut], events_ref.at[:cut], sems.at[1]),
        pltpu.make_async_copy(ids_hbm, ids_ref, sems.at[2]),
    ]
    for copy in copies:
        copy.start()
    copies[2].wait()
    ids = ids_ref[...]
    high_ref[cut:, :] = digit_rows(ids[:, cut:])
    low_ref[cut:, :] = digit_rows(ids[:, :cut])
    copies[0].wait()
    high_ref[:cut, :] = events_ref[cut:, :]
    copies[1].wait()
    low_ref[:cut, :] = events_ref[:cut, :]


def own_kernel(
    length_ref, bias_ref, events_ref, w_ref, ids_ref, gate_ref, v_ref, spread_ref, q_ref, part_ref,
    x_buf, k_buf, same_buf,
):
    rows, width = x_buf.shape
    heads, _, hd = v_ref.shape
    blocks = rows // BLOCK
    tri = triangle(True)
    spread_ids(ids_ref[...], spread_ref)
    for c in range(blocks):
        same_buf[c * BLOCK :, part(c)] = mark_same(spread_ref, slice(c * BLOCK, rows), ids_ref[:, part(c)])
    x_buf[...] = events_ref[...] * jnp.bfloat16(0.5)
    pos = lax.axis_index("hist") * rows + lax.broadcasted_iota(jnp.int32, (rows, 1), 0)

    def emit(at, y):
        kind, at = at // width, at % width
        if kind == 0:
            gate_ref[:, at : at + y.shape[1]] = y
        elif kind == 1:
            put_heads(v_ref, at, jnp.where(pos < length_ref[0], y, 0.0), hd)
        elif kind == 2:
            put_heads(q_ref, at, y * (0.5 / math.sqrt(hd)), hd)
        else:
            put_heads(k_buf, at, y, hd)

    columns(x_buf, w_ref, 0, 4 * width, emit)
    for h in range(heads):
        for c in range(blocks):
            rs = slice(c * BLOCK, rows)
            term = mixed_term(
                q_ref[h, rs, :], k_buf[h, part(c), :], v_ref[h, part(c), :], same_buf[rs, part(c)],
                0.5 * bias_ref[h], tri, 0,
            )
            part_ref[h, rs, :] = term if c == 0 else part_ref[h, rs, :] + term


def halo_piece(first, length, bias_ref, got_ref, w_ref, spread_ref, q_ref, part_ref, x_buf, k_buf, v_buf, same_buf, mix_ref):
    heads, _, hd = q_ref.shape
    keys, width = x_buf.shape
    blocks = keys // BLOCK
    tri = triangle(False)
    x_buf[...] = got_ref[:keys, :] * jnp.bfloat16(0.5)
    ids = from_digits(got_ref[keys:, :])
    for c in range(blocks):
        end = (first + c + 1) * BLOCK
        same_buf[:end, part(c)] = mark_same(spread_ref, slice(0, end), ids[:, part(c)])
    pos = lax.axis_index("hist") * WINDOW - WINDOW + first * BLOCK + lax.broadcasted_iota(jnp.int32, (keys, 1), 0)

    def emit(at, y):
        if at < 2 * width:
            put_heads(v_buf, at - width, jnp.where((pos >= 0) & (pos < length), y, 0.0), hd)
        else:
            put_heads(k_buf, at - 3 * width, y, hd)

    columns(x_buf, w_ref, width, width, emit)
    columns(x_buf, w_ref, 3 * width, width, emit)
    for h in range(heads):
        for c in range(blocks - 1, -1, -1):
            rs = slice(0, (first + c + 1) * BLOCK)
            term = mixed_term(
                q_ref[h, rs, :], k_buf[h, part(c), :], v_buf[h, part(c), :], same_buf[rs, part(c)],
                0.5 * bias_ref[h], tri, (first + c) * BLOCK,
            )
            mix_ref[h, rs, :] = (part_ref if c == blocks - 1 else mix_ref)[h, rs, :] + term


def gated_sum(first, rows, length, mix_ref, gate_ref, gated_buf):
    heads, _, hd = mix_ref.shape
    width = heads * hd

    def norm_rows(b, carry):
        at = pl.multiple_of(b * NORM_ROWS, NORM_ROWS)
        rs = pl.ds(first + at, NORM_ROWS)
        mixed = [mix_ref[h, rs, :] for h in range(heads)]
        mean = jnp.sum(sum(mixed), axis=1, keepdims=True) * (1.0 / width)
        mixed = [m - mean for m in mixed]
        spread = jnp.sum(sum(m * m for m in mixed), axis=1, keepdims=True) * (1.0 / width)
        factor = lax.rsqrt(spread + 1e-06 * WINDOW * WINDOW)
        for h in range(heads):
            gated = mixed[h] * factor * gate_ref[rs, h * hd : (h + 1) * hd]
            gated_buf[pl.ds(at, NORM_ROWS), h * hd : (h + 1) * hd] = gated.astype(jnp.bfloat16)
        return carry

    lax.fori_loop(0, rows // NORM_ROWS, norm_rows, 0, unroll=NORM_UNROLL)
    return mm(valid(first, rows, length), gated_buf[...])


def valid(first, rows, length):
    place = lax.axis_index("hist") * WINDOW + first + lax.broadcasted_iota(jnp.int32, (8, rows), 1)
    return jnp.where(place < length, 1.0, 0.0).astype(jnp.bfloat16)


def high_kernel(
    length_ref, bias_ref, got_ref, w_ref, spread_ref, q_ref, part_ref, gate_ref, events_ref,
    mix_ref, sums_ref, x_buf, k_buf, v_buf, same_buf, gated_buf,
):
    rows = q_ref.shape[1]
    cut = rows // 2
    length = length_ref[0]
    halo_piece(
        cut // BLOCK, length, bias_ref, got_ref, w_ref, spread_ref, q_ref, part_ref, x_buf, k_buf, v_buf, same_buf, mix_ref
    )
    sums_ref[0] = gated_sum(cut, rows - cut, length, mix_ref, gate_ref, gated_buf)
    sums_ref[1] = mm(valid(0, rows, length), events_ref[...])


def low_kernel(
    length_ref, bias_ref, got_ref, w_ref, spread_ref, q_ref, part_ref, gate_ref, sums_ref, w_out_ref,
    out_ref, x_buf, k_buf, v_buf, same_buf, mix_buf, gated_buf,
):
    cut = gated_buf.shape[0]
    length = length_ref[0]
    halo_piece(0, length, bias_ref, got_ref, w_ref, spread_ref, q_ref, part_ref, x_buf, k_buf, v_buf, same_buf, mix_buf)
    total = sums_ref[0] + gated_sum(0, cut, length, mix_buf, gate_ref, gated_buf)
    high = total.astype(jnp.bfloat16).astype(jnp.float32)
    middle = (total - high).astype(jnp.bfloat16).astype(jnp.float32)
    low = total - high - middle
    which = lax.broadcasted_iota(jnp.int32, total.shape, 0)
    terms = jnp.where(which == 0, high, jnp.where(which == 1, middle, jnp.where(which == 2, low, 0.0)))
    projected = jnp.sum(mm(terms.astype(jnp.bfloat16), w_out_ref[...]), axis=0, keepdims=True)
    pooled = projected + sums_ref[1][:1]
    for j in range(out_ref.shape[0]):
        out_ref[j] = pooled


NORM_ROWS = 32
NORM_UNROLL = 4


SMEM = pl.BlockSpec(memory_space=pltpu.SMEM)
VMEM = pl.BlockSpec(memory_space=pltpu.VMEM)


def shifted(block, axis, distance):
    devices = range(lax.axis_size(axis))
    route = [(i - distance, i) for i in devices if i - distance in devices]
    return lax.ppermute(block, axis, route)


HBM = pl.BlockSpec(memory_space=pltpu.MemorySpace.HBM)


def kernel_call(kernel, outs, specs, scratch, args, mflops):
    return pl.pallas_call(
        kernel,
        out_shape=outs,
        in_specs=specs,
        out_specs=jax.tree.map(lambda _: VMEM, outs),
        scratch_shapes=scratch,
        compiler_params=pltpu.CompilerParams(vmem_limit_bytes=24 << 20),
        cost_estimate=pl.CostEstimate(flops=mflops * 10**6, bytes_accessed=10**7, transcendentals=10**6),
    )(*args)


def local_pool(events, item_ids, lengths, w_proj, w_out, repeat_bias):
    _, rows, width = events.shape
    heads = repeat_bias.shape[0]
    hd = width // heads
    cut = rows // 2
    bf16 = functools.partial(jax.ShapeDtypeStruct, dtype=jnp.bfloat16)
    f32 = functools.partial(jax.ShapeDtypeStruct, dtype=jnp.float32)
    stay = [pltpu.with_memory_space_constraint(a, pltpu.MemorySpace.HBM) for a in (events, item_ids)]
    high, low, x = kernel_call(
        send_kernel, (bf16((cut + 16, width)), bf16((cut + 16, width)), bf16((rows, width))), [HBM] * 2,
        [pltpu.VMEM(item_ids.shape, jnp.int32), pltpu.SemaphoreType.DMA((3,))], stay, 4000,
    )
    high = shifted(high, "hist", 1)
    low = shifted(low, "hist", 1)
    gate, _, spread, q, mixed = kernel_call(
        own_kernel,
        (
            f32((rows, width)), bf16((heads, rows, hd)), jax.ShapeDtypeStruct((rows, 128), jnp.int32),
            bf16((heads, rows, hd)), f32((heads, rows, hd)),
        ),
        [SMEM] * 2 + [VMEM] * 3,
        [
            pltpu.VMEM((rows, width), jnp.bfloat16), pltpu.VMEM((heads, rows, hd), jnp.bfloat16),
            pltpu.VMEM((rows, rows), jnp.float32),
        ],
        (lengths, repeat_bias, x, w_proj, item_ids), 7000,
    )
    piece = [
        pltpu.VMEM((cut, width), jnp.bfloat16),
        pltpu.VMEM((heads, cut, hd), jnp.bfloat16),
        pltpu.VMEM((heads, cut, hd), jnp.bfloat16),
    ]
    mixed, sums = kernel_call(
        high_kernel,
        (f32((heads, rows, hd)), f32((2, 8, width))),
        [SMEM] * 2 + [VMEM] * 7,
        piece + [pltpu.VMEM((rows, cut), jnp.float32), pltpu.VMEM((cut, width), jnp.bfloat16)],
        (lengths, repeat_bias, high, w_proj, spread, q, mixed, gate, x), 4000,
    )
    return kernel_call(
        low_kernel,
        f32((lax.axis_size("hist"), 1, width)),
        [SMEM] * 2 + [VMEM] * 8,
        piece + [
            pltpu.VMEM((cut, cut), jnp.float32), pltpu.VMEM((heads, cut, hd), jnp.float32),
            pltpu.VMEM((cut, width), jnp.bfloat16),
        ],
        (lengths, repeat_bias, low, w_proj, spread, q, mixed, gate, sums, w_out), 2000,
    )


def vector_kernel(parts_ref, out_ref):
    pooled = parts_ref[0]
    for j in range(1, parts_ref.shape[0]):
        pooled = pooled + parts_ref[j]
    normed = pooled * lax.rsqrt(jnp.mean(pooled * pooled, axis=1, keepdims=True) + 1e-06)
    normed = normed.astype(jnp.bfloat16).astype(jnp.float32)
    for j in range(out_ref.shape[0]):
        out_ref[j] = normed


def as_row(column):
    users = column.shape[0]
    square = jnp.concatenate(
        [jnp.broadcast_to(column, (users, 128)), jnp.zeros((128 - users, 128), jnp.float32)], axis=0
    )
    return square.T[:1]


def logit_kernel(vecs_ref, slab_ref, logits_ref, lse_ref):
    vecs = jnp.concatenate([vecs_ref[j] for j in range(vecs_ref.shape[0])], axis=0).astype(jnp.bfloat16)
    logits = 4.0 * lax.dot_general(vecs, slab_ref[...], NT, preferred_element_type=jnp.float32)
    logits_ref[...] = logits
    top = jnp.max(logits, axis=1, keepdims=True)
    lse = top + jnp.log(jnp.sum(jnp.exp(logits - top), axis=1, keepdims=True))
    row = as_row(lse)
    for j in range(lse_ref.shape[0]):
        lse_ref[j] = row


def joined(parts_ref):
    parts = [parts_ref[j] for j in range(parts_ref.shape[0])]
    top = functools.reduce(jnp.maximum, parts)
    return top + jnp.log(sum(jnp.exp(p - top) for p in parts))


def join_kernel(parts_ref, out_ref):
    lse = joined(parts_ref)
    for j in range(out_ref.shape[0]):
        out_ref[j] = lse


def final_kernel(parts_ref, logits_ref, out_ref):
    users = logits_ref.shape[0]
    lse = jnp.broadcast_to(joined(parts_ref), (128, 128)).T[:users, :1]
    out_ref[...] = logits_ref[...] - lse


def small(kernel, outs, *args):
    return pl.pallas_call(
        kernel,
        out_shape=outs,
        in_specs=[VMEM] * len(args),
        out_specs=jax.tree.map(lambda _: VMEM, outs),
        compiler_params=pltpu.CompilerParams(vmem_limit_bytes=16 << 20),
    )(*args)


def swapped(x, axis):
    return lax.all_to_all(x, axis, 0, 0, tiled=True)


def local(events, item_ids, lengths, w_proj, w_out, repeat_bias, item_slab):
    f32 = functools.partial(jax.ShapeDtypeStruct, dtype=jnp.float32)
    hists, items = lax.axis_size("hist"), lax.axis_size("item")
    users, width = items * events.shape[0], events.shape[2]
    parts = local_pool(events, item_ids, lengths, w_proj, w_out, repeat_bias)
    vecs = small(vector_kernel, f32((items, 1, width)), swapped(parts, "hist"))
    logits, lse = small(
        logit_kernel, (f32((users, item_slab.shape[0])), f32((hists, 1, 128))),
        swapped(vecs, "item"), item_slab,
    )
    lse = small(join_kernel, f32((items, 1, 128)), swapped(lse, "hist"))
    return small(final_kernel, f32(logits.shape), swapped(lse, "item"), logits)


def solution(mesh):
    placed = (
        P("item", "hist", None),
        P("item", "hist"),
        P("item"),
        P(),
        P(),
        P(),
        P(("hist", "item"), None),
    )
    return jax.shard_map(
        local, mesh=mesh, in_specs=placed, out_specs=P(None, ("hist", "item")), check_vma=False
    )
```

```python
import functools
import math

import jax
import jax.numpy as jnp
from jax import lax
from jax.experimental import pallas as pl
from jax.experimental.pallas import tpu as pltpu
from jax.sharding import PartitionSpec as P


WINDOW = 1024
BLOCK = 256
NT = (((1,), (1,)), ((), ()))


def mm(a, b):
    return jnp.dot(a, b, preferred_element_type=jnp.float32)


def spread_ids(row, out_ref):
    for b in range(out_ref.shape[0] // 128):
        out_ref[b * 128 : (b + 1) * 128, :] = jnp.broadcast_to(row[:, b * 128 : (b + 1) * 128], (128, 128)).T


def part(b):
    return slice(b * BLOCK, (b + 1) * BLOCK)


def mark_same(spread, rows, ids):
    mine = jnp.concatenate([spread[rows, :]] * (ids.shape[1] // 128), axis=1)
    return jnp.where(mine == ids, 1.0, 0.0)


def triangle(below):
    row = lax.broadcasted_iota(jnp.int32, (BLOCK, BLOCK), 0)
    col = lax.broadcasted_iota(jnp.int32, (BLOCK, BLOCK), 1)
    return jnp.where((col <= row) if below else (col > row), 1.0, 0.0).astype(jnp.bfloat16)


def mixed_term(q, k, v, same, bias, tri, at):
    half = lax.dot_general(q, k, NT, preferred_element_type=jnp.float32) + same * bias
    weights = (half * jnp.tanh(half) + half).astype(jnp.bfloat16)
    pieces = [weights[:at], weights[at : at + BLOCK] * tri, weights[at + BLOCK :]]
    pieces = [p for p in pieces if p.shape[0]]
    return mm(jnp.concatenate(pieces, axis=0) if len(pieces) > 1 else pieces[0], v)


def columns(x_ref, w_ref, first, count, emit):
    for at in range(first, first + count, 256):
        half = mm(x_ref[...], w_ref[:, at : at + 256])
        emit(at, half * jnp.tanh(half) + half)


def put_heads(buf, at, y, hd):
    y = y.astype(jnp.bfloat16)
    for h in range(y.shape[1] // hd):
        buf[at // hd + h] = y[:, h * hd : (h + 1) * hd]


def digit_rows(ids):
    which = lax.broadcasted_iota(jnp.int32, (16, ids.shape[1]), 0)
    digits = jnp.where(which == 0, ids & 127, jnp.where(which == 1, (ids >> 7) & 127, ids >> 14))
    return jnp.where(which < 3, digits, 0).astype(jnp.float32).astype(jnp.bfloat16)


def from_digits(rows):
    rows = rows.astype(jnp.float32)
    return (rows[0:1] + 128.0 * rows[1:2] + 16384.0 * rows[2:3]).astype(jnp.int32)


def send_kernel(first, x_hbm, ids_hbm, out_ref, ids_ref, sems):
    cut = ids_ref.shape[1] // 2
    copies = [
        pltpu.make_async_copy(x_hbm.at[0, first : first + cut], out_ref.at[:cut], sems.at[0]),
        pltpu.make_async_copy(ids_hbm, ids_ref, sems.at[1]),
    ]
    for copy in copies:
        copy.start()
    copies[1].wait()
    out_ref[cut:, :] = digit_rows(ids_ref[:, first : first + cut])
    copies[0].wait()


def own_kernel(
    length_ref, bias_ref, high_ref, low_ref, w_ref, ids_ref, gate_ref, v_ref, spread_ref, q_ref, part_ref,
    x_buf, k_buf, same_buf,
):
    rows, width = x_buf.shape
    heads, _, hd = v_ref.shape
    blocks = rows // BLOCK
    tri = triangle(True)
    spread_ids(ids_ref[...], spread_ref)
    for c in range(blocks):
        same_buf[c * BLOCK :, part(c)] = mark_same(spread_ref, slice(c * BLOCK, rows), ids_ref[:, part(c)])
    cut = rows // 2
    x_buf[:cut, :] = low_ref[:cut, :] * jnp.bfloat16(0.5)
    x_buf[cut:, :] = high_ref[:cut, :] * jnp.bfloat16(0.5)
    pos = lax.axis_index("hist") * rows + lax.broadcasted_iota(jnp.int32, (rows, 1), 0)

    def emit(at, y):
        kind, at = at // width, at % width
        if kind == 0:
            gate_ref[:, at : at + y.shape[1]] = y
        elif kind == 1:
            put_heads(v_ref, at, jnp.where(pos < length_ref[:1, :1], y, 0.0), hd)
        elif kind == 2:
            put_heads(q_ref, at, y * (0.5 / math.sqrt(hd)), hd)
        else:
            put_heads(k_buf, at, y, hd)

    columns(x_buf, w_ref, 0, 4 * width, emit)
    for h in range(heads):
        for c in range(blocks):
            rs = slice(c * BLOCK, rows)
            term = mixed_term(
                q_ref[h, rs, :], k_buf[h, part(c), :], v_ref[h, part(c), :], same_buf[rs, part(c)],
                0.5 * bias_ref[h], tri, 0,
            )
            part_ref[h, rs, :] = term if c == 0 else part_ref[h, rs, :] + term


def halo_piece(first, length, bias_ref, got_ref, w_ref, spread_ref, q_ref, part_ref, x_buf, k_buf, v_buf, same_buf, mix_ref):
    heads, _, hd = q_ref.shape
    keys, width = x_buf.shape
    blocks = keys // BLOCK
    tri = triangle(False)
    x_buf[...] = got_ref[:keys, :] * jnp.bfloat16(0.5)
    ids = from_digits(got_ref[keys:, :])
    for c in range(blocks):
        end = (first + c + 1) * BLOCK
        same_buf[:end, part(c)] = mark_same(spread_ref, slice(0, end), ids[:, part(c)])
    pos = lax.axis_index("hist") * WINDOW - WINDOW + first * BLOCK + lax.broadcasted_iota(jnp.int32, (keys, 1), 0)

    def emit(at, y):
        if at < 2 * width:
            put_heads(v_buf, at - width, jnp.where((pos >= 0) & (pos < length), y, 0.0), hd)
        else:
            put_heads(k_buf, at - 3 * width, y, hd)

    columns(x_buf, w_ref, width, width, emit)
    columns(x_buf, w_ref, 3 * width, width, emit)
    for h in range(heads):
        for c in range(blocks - 1, -1, -1):
            rs = slice(0, (first + c + 1) * BLOCK)
            term = mixed_term(
                q_ref[h, rs, :], k_buf[h, part(c), :], v_buf[h, part(c), :], same_buf[rs, part(c)],
                0.5 * bias_ref[h], tri, (first + c) * BLOCK,
            )
            mix_ref[h, rs, :] = (part_ref if c == blocks - 1 else mix_ref)[h, rs, :] + term


def gated_sum(first, rows, length, mix_ref, gate_ref, gated_buf):
    heads, _, hd = mix_ref.shape
    width = heads * hd

    for at in range(0, rows, NORM_ROWS):
        rs = slice(first + at, first + at + NORM_ROWS)
        mixed = [mix_ref[h, rs, :] for h in range(heads)]
        mean = jnp.sum(sum(mixed), axis=1, keepdims=True) * (1.0 / width)
        mixed = [m - mean for m in mixed]
        spread = jnp.sum(sum(m * m for m in mixed), axis=1, keepdims=True) * (1.0 / width)
        factor = lax.rsqrt(spread + 1e-06 * WINDOW * WINDOW)
        for h in range(heads):
            gated = mixed[h] * factor * gate_ref[rs, h * hd : (h + 1) * hd]
            gated_buf[at : at + NORM_ROWS, h * hd : (h + 1) * hd] = gated.astype(jnp.bfloat16)
    return mm(valid(first, rows, length), gated_buf[...])


def valid(first, rows, length):
    place = lax.axis_index("hist") * WINDOW + first + lax.broadcasted_iota(jnp.int32, (8, rows), 1)
    return jnp.where(place < length, 1.0, 0.0).astype(jnp.bfloat16)


def high_kernel(
    length_ref, bias_ref, got_ref, w_ref, spread_ref, q_ref, part_ref, gate_ref, high_ref, low_ref,
    mix_ref, sums_ref, x_buf, k_buf, v_buf, same_buf, gated_buf,
):
    rows = q_ref.shape[1]
    cut = rows // 2
    length = length_ref[:1, :1]
    halo_piece(
        cut // BLOCK, length, bias_ref, got_ref, w_ref, spread_ref, q_ref, part_ref, x_buf, k_buf, v_buf, same_buf, mix_ref
    )
    sums_ref[0] = gated_sum(cut, rows - cut, length, mix_ref, gate_ref, gated_buf)
    sums_ref[1] = mm(valid(0, cut, length), low_ref[:cut, :]) + mm(valid(cut, cut, length), high_ref[:cut, :])


def low_kernel(
    length_ref, bias_ref, got_ref, w_ref, spread_ref, q_ref, part_ref, gate_ref, sums_ref, w_out_ref,
    out_ref, x_buf, k_buf, v_buf, same_buf, mix_buf, gated_buf,
):
    cut = gated_buf.shape[0]
    length = length_ref[:1, :1]
    halo_piece(0, length, bias_ref, got_ref, w_ref, spread_ref, q_ref, part_ref, x_buf, k_buf, v_buf, same_buf, mix_buf)
    total = sums_ref[0] + gated_sum(0, cut, length, mix_buf, gate_ref, gated_buf)
    high = total.astype(jnp.bfloat16).astype(jnp.float32)
    middle = (total - high).astype(jnp.bfloat16).astype(jnp.float32)
    low = total - high - middle
    which = lax.broadcasted_iota(jnp.int32, total.shape, 0)
    terms = jnp.where(which == 0, high, jnp.where(which == 1, middle, jnp.where(which == 2, low, 0.0)))
    projected = jnp.sum(mm(terms.astype(jnp.bfloat16), w_out_ref[...]), axis=0, keepdims=True)
    pooled = projected + sums_ref[1][:1]
    for j in range(out_ref.shape[0]):
        out_ref[j] = pooled


NORM_ROWS = 32


SMEM = pl.BlockSpec(memory_space=pltpu.SMEM)
VMEM = pl.BlockSpec(memory_space=pltpu.VMEM)


def shifted(block, axis, distance):
    devices = range(lax.axis_size(axis))
    route = [(i - distance, i) for i in devices if i - distance in devices]
    return lax.ppermute(block, axis, route)


HBM = pl.BlockSpec(memory_space=pltpu.MemorySpace.HBM)


def kernel_call(kernel, outs, specs, scratch, args, mflops):
    return pl.pallas_call(
        kernel,
        out_shape=outs,
        in_specs=specs,
        out_specs=jax.tree.map(lambda _: VMEM, outs),
        scratch_shapes=scratch,
        compiler_params=pltpu.CompilerParams(vmem_limit_bytes=24 << 20),
        cost_estimate=pl.CostEstimate(flops=mflops * 10**6, bytes_accessed=10**7, transcendentals=10**6),
    )(*args)


def local_pool(events, item_ids, lengths, w_proj, w_out, repeat_bias):
    _, rows, width = events.shape
    heads = repeat_bias.shape[0]
    hd = width // heads
    cut = rows // 2
    bf16 = functools.partial(jax.ShapeDtypeStruct, dtype=jnp.bfloat16)
    f32 = functools.partial(jax.ShapeDtypeStruct, dtype=jnp.float32)
    stay = [pltpu.with_memory_space_constraint(a, pltpu.MemorySpace.HBM) for a in (events, item_ids)]

    def send(first, mflops):
        return kernel_call(
            functools.partial(send_kernel, first), bf16((cut + 16, width)), [HBM] * 2,
            [pltpu.VMEM(item_ids.shape, jnp.int32), pltpu.SemaphoreType.DMA((2,))], stay, mflops,
        )

    length = jnp.broadcast_to(lengths[:, None], (8, 128))
    own_high = send(cut, 2000)
    high = shifted(own_high, "hist", 1)
    own_low = send(0, 2000)
    low = shifted(own_low, "hist", 1)
    gate, _, spread, q, mixed = kernel_call(
        own_kernel,
        (
            f32((rows, width)), bf16((heads, rows, hd)), jax.ShapeDtypeStruct((rows, 128), jnp.int32),
            bf16((heads, rows, hd)), f32((heads, rows, hd)),
        ),
        [VMEM, SMEM] + [VMEM] * 4,
        [
            pltpu.VMEM((rows, width), jnp.bfloat16), pltpu.VMEM((heads, rows, hd), jnp.bfloat16),
            pltpu.VMEM((rows, rows), jnp.float32),
        ],
        (length, repeat_bias, own_high, own_low, w_proj, item_ids), 7000,
    )
    piece = [
        pltpu.VMEM((cut, width), jnp.bfloat16),
        pltpu.VMEM((heads, cut, hd), jnp.bfloat16),
        pltpu.VMEM((heads, cut, hd), jnp.bfloat16),
    ]
    mixed, sums = kernel_call(
        high_kernel,
        (f32((heads, rows, hd)), f32((2, 8, width))),
        [VMEM, SMEM] + [VMEM] * 8,
        piece + [pltpu.VMEM((rows, cut), jnp.float32), pltpu.VMEM((cut, width), jnp.bfloat16)],
        (length, repeat_bias, high, w_proj, spread, q, mixed, gate, own_high, own_low), 4000,
    )
    return kernel_call(
        low_kernel,
        f32((lax.axis_size("hist"), 1, width)),
        [VMEM, SMEM] + [VMEM] * 8,
        piece + [
            pltpu.VMEM((cut, cut), jnp.float32), pltpu.VMEM((heads, cut, hd), jnp.float32),
            pltpu.VMEM((cut, width), jnp.bfloat16),
        ],
        (length, repeat_bias, low, w_proj, spread, q, mixed, gate, sums, w_out), 2000,
    )


def vector_kernel(parts_ref, out_ref):
    pooled = parts_ref[0]
    for j in range(1, parts_ref.shape[0]):
        pooled = pooled + parts_ref[j]
    normed = pooled * lax.rsqrt(jnp.mean(pooled * pooled, axis=1, keepdims=True) + 1e-06)
    normed = normed.astype(jnp.bfloat16).astype(jnp.float32)
    for j in range(out_ref.shape[0]):
        out_ref[j] = normed


def as_row(column):
    users = column.shape[0]
    square = jnp.concatenate(
        [jnp.broadcast_to(column, (users, 128)), jnp.zeros((128 - users, 128), jnp.float32)], axis=0
    )
    return square.T[:1]


def logit_kernel(vecs_ref, slab_ref, logits_ref, lse_ref):
    vecs = jnp.concatenate([vecs_ref[j] for j in range(vecs_ref.shape[0])], axis=0).astype(jnp.bfloat16)
    logits = 4.0 * lax.dot_general(vecs, slab_ref[...], NT, preferred_element_type=jnp.float32)
    logits_ref[...] = logits
    top = jnp.max(logits, axis=1, keepdims=True)
    lse = top + jnp.log(jnp.sum(jnp.exp(logits - top), axis=1, keepdims=True))
    row = as_row(lse)
    for j in range(lse_ref.shape[0]):
        lse_ref[j] = row


def joined(parts_ref):
    parts = [parts_ref[j] for j in range(parts_ref.shape[0])]
    top = functools.reduce(jnp.maximum, parts)
    return top + jnp.log(sum(jnp.exp(p - top) for p in parts))


def join_kernel(parts_ref, out_ref):
    lse = joined(parts_ref)
    for j in range(out_ref.shape[0]):
        out_ref[j] = lse


def final_kernel(parts_ref, logits_ref, out_ref):
    users = logits_ref.shape[0]
    lse = jnp.broadcast_to(joined(parts_ref), (128, 128)).T[:users, :1]
    out_ref[...] = logits_ref[...] - lse


def small(kernel, outs, *args):
    return pl.pallas_call(
        kernel,
        out_shape=outs,
        in_specs=[VMEM] * len(args),
        out_specs=jax.tree.map(lambda _: VMEM, outs),
        compiler_params=pltpu.CompilerParams(vmem_limit_bytes=16 << 20),
    )(*args)


def swapped(x, axis):
    return lax.all_to_all(x, axis, 0, 0, tiled=True)


def local(events, item_ids, lengths, w_proj, w_out, repeat_bias, item_slab):
    f32 = functools.partial(jax.ShapeDtypeStruct, dtype=jnp.float32)
    hists, items = lax.axis_size("hist"), lax.axis_size("item")
    users, width = items * events.shape[0], events.shape[2]
    parts = local_pool(events, item_ids, lengths, w_proj, w_out, repeat_bias)
    vecs = small(vector_kernel, f32((items, 1, width)), swapped(parts, "hist"))
    logits, lse = small(
        logit_kernel, (f32((users, item_slab.shape[0])), f32((hists, 1, 128))),
        swapped(vecs, "item"), item_slab,
    )
    lse = small(join_kernel, f32((items, 1, 128)), swapped(lse, "hist"))
    return small(final_kernel, f32(logits.shape), swapped(lse, "item"), logits)


def solution(mesh):
    placed = (
        P("item", "hist", None),
        P("item", "hist"),
        P("item"),
        P(),
        P(),
        P(),
        P(("hist", "item"), None),
    )
    return jax.shard_map(
        local, mesh=mesh, in_specs=placed, out_specs=P(None, ("hist", "item")), check_vma=False
    )
```

```python
import functools
import math

import jax
import jax.numpy as jnp
from jax import lax
from jax.experimental import pallas as pl
from jax.experimental.pallas import tpu as pltpu
from jax.sharding import PartitionSpec as P


WINDOW = 1024
BLOCK = 256
NT = (((1,), (1,)), ((), ()))


def mm(a, b):
    return jnp.dot(a, b, preferred_element_type=jnp.float32)


def spread_ids(row, out_ref):
    for b in range(out_ref.shape[0] // 128):
        out_ref[b * 128 : (b + 1) * 128, :] = jnp.broadcast_to(row[:, b * 128 : (b + 1) * 128], (128, 128)).T


def part(b):
    return slice(b * BLOCK, (b + 1) * BLOCK)


def mark_same(spread, rows, ids):
    mine = jnp.concatenate([spread[rows, :]] * (ids.shape[1] // 128), axis=1)
    return jnp.where(mine == ids, 1.0, 0.0)


def spread_length(length_ref, rows, lanes):
    tile = jnp.concatenate([length_ref[...]] * (lanes // 128), axis=1)
    return jnp.concatenate([tile] * (rows // 8), axis=0) if rows > 8 else tile


def triangle(below):
    row = lax.broadcasted_iota(jnp.int32, (BLOCK, BLOCK), 0)
    col = lax.broadcasted_iota(jnp.int32, (BLOCK, BLOCK), 1)
    return jnp.where((col <= row) if below else (col > row), 1.0, 0.0).astype(jnp.bfloat16)


def mixed_term(q, k, v, same, bias, tri, at):
    half = lax.dot_general(q, k, NT, preferred_element_type=jnp.float32) + same * bias
    weights = (half * jnp.tanh(half) + half).astype(jnp.bfloat16)
    pieces = [weights[:at], weights[at : at + BLOCK] * tri, weights[at + BLOCK :]]
    pieces = [p for p in pieces if p.shape[0]]
    return mm(jnp.concatenate(pieces, axis=0) if len(pieces) > 1 else pieces[0], v)


def columns(x_ref, w_ref, first, count, emit):
    for at in range(first, first + count, 256):
        half = mm(x_ref[...], w_ref[:, at : at + 256])
        emit(at, half * jnp.tanh(half) + half)


def put_heads(buf, at, y, hd):
    y = y.astype(jnp.bfloat16)
    for h in range(y.shape[1] // hd):
        buf[at // hd + h] = y[:, h * hd : (h + 1) * hd]


def digit_rows(ids):
    which = lax.broadcasted_iota(jnp.int32, (16, ids.shape[1]), 0)
    digits = jnp.where(which == 0, ids & 127, jnp.where(which == 1, (ids >> 7) & 127, ids >> 14))
    return jnp.where(which < 3, digits, 0).astype(jnp.float32).astype(jnp.bfloat16)


def from_digits(rows):
    rows = rows.astype(jnp.float32)
    return (rows[0:1] + 128.0 * rows[1:2] + 16384.0 * rows[2:3]).astype(jnp.int32)


def send_kernel(first, x_hbm, ids_hbm, out_ref, ids_ref, sems):
    cut = ids_ref.shape[1] // 2
    copies = [
        pltpu.make_async_copy(x_hbm.at[0, first : first + cut], out_ref.at[:cut], sems.at[0]),
        pltpu.make_async_copy(ids_hbm, ids_ref, sems.at[1]),
    ]
    for copy in copies:
        copy.start()
    copies[1].wait()
    out_ref[cut:, :] = digit_rows(ids_ref[:, first : first + cut])
    copies[0].wait()


def own_kernel(
    length_ref, bias_ref, high_ref, low_ref, w_ref, ids_ref, gate_ref, v_ref, spread_ref, q_ref, part_ref,
    x_buf, k_buf, same_buf,
):
    rows, width = x_buf.shape
    heads, _, hd = v_ref.shape
    blocks = rows // BLOCK
    tri = triangle(True)
    spread_ids(ids_ref[...], spread_ref)
    for c in range(blocks):
        same_buf[c * BLOCK :, part(c)] = mark_same(spread_ref, slice(c * BLOCK, rows), ids_ref[:, part(c)])
    cut = rows // 2
    x_buf[:cut, :] = low_ref[:cut, :] * jnp.bfloat16(0.5)
    x_buf[cut:, :] = high_ref[:cut, :] * jnp.bfloat16(0.5)
    pos = lax.axis_index("hist") * rows + lax.broadcasted_iota(jnp.int32, (rows, 256), 0)

    def emit(at, y):
        kind, at = at // width, at % width
        if kind == 0:
            gate_ref[:, at : at + y.shape[1]] = y
        elif kind == 1:
            put_heads(v_ref, at, jnp.where(pos < spread_length(length_ref, rows, 256), y, 0.0), hd)
        elif kind == 2:
            put_heads(q_ref, at, y * (0.5 / math.sqrt(hd)), hd)
        else:
            put_heads(k_buf, at, y, hd)

    columns(x_buf, w_ref, 0, 4 * width, emit)
    for h in range(heads):
        for c in range(blocks):
            rs = slice(c * BLOCK, rows)
            term = mixed_term(
                q_ref[h, rs, :], k_buf[h, part(c), :], v_ref[h, part(c), :], same_buf[rs, part(c)],
                0.5 * bias_ref[h], tri, 0,
            )
            part_ref[h, rs, :] = term if c == 0 else part_ref[h, rs, :] + term


def halo_piece(first, length_ref, bias_ref, got_ref, w_ref, spread_ref, q_ref, part_ref, x_buf, k_buf, v_buf, same_buf, mix_ref):
    heads, _, hd = q_ref.shape
    keys, width = x_buf.shape
    blocks = keys // BLOCK
    tri = triangle(False)
    x_buf[...] = got_ref[:keys, :] * jnp.bfloat16(0.5)
    ids = from_digits(got_ref[keys:, :])
    for c in range(blocks):
        end = (first + c + 1) * BLOCK
        same_buf[:end, part(c)] = mark_same(spread_ref, slice(0, end), ids[:, part(c)])
    pos = lax.axis_index("hist") * WINDOW - WINDOW + first * BLOCK + lax.broadcasted_iota(jnp.int32, (keys, 256), 0)

    def emit(at, y):
        if at < 2 * width:
            put_heads(v_buf, at - width, jnp.where((pos >= 0) & (pos < spread_length(length_ref, keys, 256)), y, 0.0), hd)
        else:
            put_heads(k_buf, at - 3 * width, y, hd)

    columns(x_buf, w_ref, width, width, emit)
    columns(x_buf, w_ref, 3 * width, width, emit)
    for h in range(heads):
        for c in range(blocks - 1, -1, -1):
            rs = slice(0, (first + c + 1) * BLOCK)
            term = mixed_term(
                q_ref[h, rs, :], k_buf[h, part(c), :], v_buf[h, part(c), :], same_buf[rs, part(c)],
                0.5 * bias_ref[h], tri, (first + c) * BLOCK,
            )
            mix_ref[h, rs, :] = (part_ref if c == blocks - 1 else mix_ref)[h, rs, :] + term


def gated_sum(first, rows, length_ref, mix_ref, gate_ref, gated_buf):
    heads, _, hd = mix_ref.shape
    width = heads * hd

    for at in range(0, rows, NORM_ROWS):
        rs = slice(first + at, first + at + NORM_ROWS)
        mixed = [mix_ref[h, rs, :] for h in range(heads)]
        mean = jnp.sum(sum(mixed), axis=1, keepdims=True) * (1.0 / width)
        mixed = [m - mean for m in mixed]
        spread = jnp.sum(sum(m * m for m in mixed), axis=1, keepdims=True) * (1.0 / width)
        factor = lax.rsqrt(spread + 1e-06 * WINDOW * WINDOW)
        for h in range(heads):
            gated = mixed[h] * factor * gate_ref[rs, h * hd : (h + 1) * hd]
            gated_buf[at : at + NORM_ROWS, h * hd : (h + 1) * hd] = gated.astype(jnp.bfloat16)
    return mm(valid(first, rows, length_ref), gated_buf[...])


def valid(first, rows, length_ref):
    place = lax.axis_index("hist") * WINDOW + first + lax.broadcasted_iota(jnp.int32, (8, rows), 1)
    return jnp.where(place < spread_length(length_ref, 8, rows), 1.0, 0.0).astype(jnp.bfloat16)


def high_kernel(
    length_ref, bias_ref, got_ref, w_ref, spread_ref, q_ref, part_ref, gate_ref, high_ref, low_ref,
    mix_ref, sums_ref, x_buf, k_buf, v_buf, same_buf, gated_buf,
):
    rows = q_ref.shape[1]
    cut = rows // 2
    halo_piece(
        cut // BLOCK, length_ref, bias_ref, got_ref, w_ref, spread_ref, q_ref, part_ref, x_buf, k_buf, v_buf, same_buf, mix_ref
    )
    sums_ref[0] = gated_sum(cut, rows - cut, length_ref, mix_ref, gate_ref, gated_buf)
    sums_ref[1] = mm(valid(0, cut, length_ref), low_ref[:cut, :]) + mm(valid(cut, cut, length_ref), high_ref[:cut, :])


def low_kernel(
    length_ref, bias_ref, got_ref, w_ref, spread_ref, q_ref, part_ref, gate_ref, sums_ref, w_out_ref,
    out_ref, x_buf, k_buf, v_buf, same_buf, mix_buf, gated_buf,
):
    cut = gated_buf.shape[0]
    halo_piece(0, length_ref, bias_ref, got_ref, w_ref, spread_ref, q_ref, part_ref, x_buf, k_buf, v_buf, same_buf, mix_buf)
    total = sums_ref[0] + gated_sum(0, cut, length_ref, mix_buf, gate_ref, gated_buf)
    high = total.astype(jnp.bfloat16).astype(jnp.float32)
    middle = (total - high).astype(jnp.bfloat16).astype(jnp.float32)
    low = total - high - middle
    which = lax.broadcasted_iota(jnp.int32, total.shape, 0)
    terms = jnp.where(which == 0, high, jnp.where(which == 1, middle, jnp.where(which == 2, low, 0.0)))
    projected = jnp.sum(mm(terms.astype(jnp.bfloat16), w_out_ref[...]), axis=0, keepdims=True)
    pooled = projected + sums_ref[1][:1]
    for j in range(out_ref.shape[0]):
        out_ref[j] = pooled


NORM_ROWS = 32


SMEM = pl.BlockSpec(memory_space=pltpu.SMEM)
VMEM = pl.BlockSpec(memory_space=pltpu.VMEM)


def shifted(block, axis, distance):
    devices = range(lax.axis_size(axis))
    route = [(i - distance, i) for i in devices if i - distance in devices]
    return lax.ppermute(block, axis, route)


HBM = pl.BlockSpec(memory_space=pltpu.MemorySpace.HBM)


def kernel_call(kernel, outs, specs, scratch, args, mflops):
    return pl.pallas_call(
        kernel,
        out_shape=outs,
        in_specs=specs,
        out_specs=jax.tree.map(lambda _: VMEM, outs),
        scratch_shapes=scratch,
        compiler_params=pltpu.CompilerParams(vmem_limit_bytes=24 << 20),
        cost_estimate=pl.CostEstimate(flops=mflops * 10**6, bytes_accessed=10**7, transcendentals=10**6),
    )(*args)


def local_pool(events, item_ids, lengths, w_proj, w_out, repeat_bias):
    _, rows, width = events.shape
    heads = repeat_bias.shape[0]
    hd = width // heads
    cut = rows // 2
    bf16 = functools.partial(jax.ShapeDtypeStruct, dtype=jnp.bfloat16)
    f32 = functools.partial(jax.ShapeDtypeStruct, dtype=jnp.float32)
    stay = [pltpu.with_memory_space_constraint(a, pltpu.MemorySpace.HBM) for a in (events, item_ids)]

    def send(first, mflops):
        return kernel_call(
            functools.partial(send_kernel, first), bf16((cut + 16, width)), [HBM] * 2,
            [pltpu.VMEM(item_ids.shape, jnp.int32), pltpu.SemaphoreType.DMA((2,))], stay, mflops,
        )

    length = jnp.broadcast_to(lengths[:, None], (8, 128))
    own_high = send(cut, 2000)
    high = shifted(own_high, "hist", 1)
    own_low = send(0, 2000)
    low = shifted(own_low, "hist", 1)
    gate, _, spread, q, mixed = kernel_call(
        own_kernel,
        (
            f32((rows, width)), bf16((heads, rows, hd)), jax.ShapeDtypeStruct((rows, 128), jnp.int32),
            bf16((heads, rows, hd)), f32((heads, rows, hd)),
        ),
        [VMEM, SMEM] + [VMEM] * 4,
        [
            pltpu.VMEM((rows, width), jnp.bfloat16), pltpu.VMEM((heads, rows, hd), jnp.bfloat16),
            pltpu.VMEM((rows, rows), jnp.float32),
        ],
        (length, repeat_bias, own_high, own_low, w_proj, item_ids), 7000,
    )
    piece = [
        pltpu.VMEM((cut, width), jnp.bfloat16),
        pltpu.VMEM((heads, cut, hd), jnp.bfloat16),
        pltpu.VMEM((heads, cut, hd), jnp.bfloat16),
    ]
    mixed, sums = kernel_call(
        high_kernel,
        (f32((heads, rows, hd)), f32((2, 8, width))),
        [VMEM, SMEM] + [VMEM] * 8,
        piece + [pltpu.VMEM((rows, cut), jnp.float32), pltpu.VMEM((cut, width), jnp.bfloat16)],
        (length, repeat_bias, high, w_proj, spread, q, mixed, gate, own_high, own_low), 4000,
    )
    return kernel_call(
        low_kernel,
        f32((lax.axis_size("hist"), 1, width)),
        [VMEM, SMEM] + [VMEM] * 8,
        piece + [
            pltpu.VMEM((cut, cut), jnp.float32), pltpu.VMEM((heads, cut, hd), jnp.float32),
            pltpu.VMEM((cut, width), jnp.bfloat16),
        ],
        (length, repeat_bias, low, w_proj, spread, q, mixed, gate, sums, w_out), 2000,
    )


def vector_kernel(parts_ref, out_ref):
    pooled = parts_ref[0]
    for j in range(1, parts_ref.shape[0]):
        pooled = pooled + parts_ref[j]
    normed = pooled * lax.rsqrt(jnp.mean(pooled * pooled, axis=1, keepdims=True) + 1e-06)
    normed = normed.astype(jnp.bfloat16).astype(jnp.float32)
    for j in range(out_ref.shape[0]):
        out_ref[j] = normed


def as_row(column):
    users = column.shape[0]
    square = jnp.concatenate(
        [jnp.broadcast_to(column, (users, 128)), jnp.zeros((128 - users, 128), jnp.float32)], axis=0
    )
    return square.T[:1]


def logit_kernel(vecs_ref, slab_ref, logits_ref, lse_ref):
    vecs = jnp.concatenate([vecs_ref[j] for j in range(vecs_ref.shape[0])], axis=0).astype(jnp.bfloat16)
    logits = 4.0 * lax.dot_general(vecs, slab_ref[...], NT, preferred_element_type=jnp.float32)
    logits_ref[...] = logits
    top = jnp.max(logits, axis=1, keepdims=True)
    lse = top + jnp.log(jnp.sum(jnp.exp(logits - top), axis=1, keepdims=True))
    row = as_row(lse)
    for j in range(lse_ref.shape[0]):
        lse_ref[j] = row


def joined(parts_ref):
    parts = [parts_ref[j] for j in range(parts_ref.shape[0])]
    top = functools.reduce(jnp.maximum, parts)
    return top + jnp.log(sum(jnp.exp(p - top) for p in parts))


def join_kernel(parts_ref, out_ref):
    lse = joined(parts_ref)
    for j in range(out_ref.shape[0]):
        out_ref[j] = lse


def final_kernel(parts_ref, logits_ref, out_ref):
    users = logits_ref.shape[0]
    lse = jnp.broadcast_to(joined(parts_ref), (128, 128)).T[:users, :1]
    out_ref[...] = logits_ref[...] - lse


def small(kernel, outs, *args):
    return pl.pallas_call(
        kernel,
        out_shape=outs,
        in_specs=[VMEM] * len(args),
        out_specs=jax.tree.map(lambda _: VMEM, outs),
        compiler_params=pltpu.CompilerParams(vmem_limit_bytes=16 << 20),
    )(*args)


def swapped(x, axis):
    return lax.all_to_all(x, axis, 0, 0, tiled=True)


def local(events, item_ids, lengths, w_proj, w_out, repeat_bias, item_slab):
    f32 = functools.partial(jax.ShapeDtypeStruct, dtype=jnp.float32)
    hists, items = lax.axis_size("hist"), lax.axis_size("item")
    users, width = items * events.shape[0], events.shape[2]
    parts = local_pool(events, item_ids, lengths, w_proj, w_out, repeat_bias)
    vecs = small(vector_kernel, f32((items, 1, width)), swapped(parts, "hist"))
    logits, lse = small(
        logit_kernel, (f32((users, item_slab.shape[0])), f32((hists, 1, 128))),
        swapped(vecs, "item"), item_slab,
    )
    lse = small(join_kernel, f32((items, 1, 128)), swapped(lse, "hist"))
    return small(final_kernel, f32(logits.shape), swapped(lse, "item"), logits)


def solution(mesh):
    placed = (
        P("item", "hist", None),
        P("item", "hist"),
        P("item"),
        P(),
        P(),
        P(),
        P(("hist", "item"), None),
    )
    return jax.shard_map(
        local, mesh=mesh, in_specs=placed, out_specs=P(None, ("hist", "item")), check_vma=False
    )
```
